128 devices in a mesh: lat: 16 (over x, z), wave: 8 (over y, core).
Axes of the slice: x: 4, y: 4, z: 4, core: 2. Of those that a mesh axis runs over, the one named last changes fastest.
Arguments:
- fourier: bfloat16 [2, 2000, 64, 256], P(None, 'lat', None, 'wave'), may hold values from -6 to 6
- table: bfloat16 [64, 2000, 4000], P('wave', 'lat'), may hold values from -0.125 to 0.125
- wavenums: int32 [64], P('wave'), may hold values from 0 to 3999, as said below
Outputs:
- spectra: float32 [4000, 64, 256], P('lat', 'wave')
The draws below stay inside these ranges and needn't reach their ends.
Inputs may be any that keep to these rules, and one draw needn't show every extreme that they name: `wavenums`: the entries are distinct and include 0 and 3999; with G = 8 groups, entry g * 8 + k is the (k * G + g)-th smallest (counting from 0).
All inputs are finite; a program needn't handle non-finite values.
Results may differ from the reference program's by a relative error of at most 0.0003.
Values may be sent and summed in bfloat16 or wider, within the bound.
No kernel may reach another device: no remote copies, remote signals or barrier semaphores. Data moves between devices by JAX's collectives and lax.ppermute only.
A program may use at most 256 MiB of HBM per device.

```python
import jax
import jax.numpy as jnp
from jax import lax

NH = 2000
NDEG = 4000
WAVE_DEV = 8
COLS = 256
WAVES = 64
N_LAT = 16


def draw_wavenums(key, part):
    inner = jax.random.permutation(key, NDEG - 2)[:WAVES - 2].astype(jnp.int32) + 1
    ends = jnp.array([0, NDEG - 1], dtype=jnp.int32)
    ordered = jnp.sort(jnp.concatenate([ends, inner]))
    groups = WAVES // WAVE_DEV
    return ordered.reshape(WAVE_DEV, groups).T.reshape(WAVES)


def strengthened(values, key, source, target, parts, factor):
    def block_of(axis_at):
        return (jnp.arange(values.shape[axis_at]) // (values.shape[axis_at] // parts)).reshape((-1,) + (1,) * (values.ndim - 1 - axis_at))

    first = jax.random.permutation(key, parts)[block_of(target)]
    second = (block_of(target) + parts // 2) % parts
    return jnp.where((block_of(source) == first) | (block_of(source) == second), factor * values, values)


def block_scale(rng, shape, split, smallest, largest):
    loudness = 1.0
    for position, blocks in split:
        steps = jax.random.uniform(jax.random.fold_in(jax.random.fold_in(rng, 6), position), (blocks,), jnp.float32, smallest / len(split), largest / len(split))
        loudness = loudness * jnp.repeat(jnp.exp(steps), shape[position] // blocks).reshape((-1,) + (1,) * (len(shape) - 1 - position))
    return loudness


def normal_values(rng, extent, scale, reach, cuts=(), held_as=jnp.bfloat16):
    level = block_scale(rng, extent, cuts, -0.22, 0.18) if cuts else 1.0
    drawn = jax.random.normal(rng, extent, jnp.float32) * scale * level
    return jnp.minimum(jnp.maximum(drawn, -reach), reach).astype(held_as)


def bell_draw_with(rng, shape, deviation, reach, pieces, heavy, kind=jnp.bfloat16):
    entries = deviation * jax.random.normal(rng, shape, jnp.float32)
    if pieces:
        entries = entries * block_scale(rng, shape, pieces, -0.22, 0.18)
    return jnp.clip(strengthened(entries, jax.random.fold_in(rng, 3), *heavy), -reach, reach).astype(kind)


def setup_inputs(seed: int = 0) -> dict:
    streams_of = jax.random.split(jax.random.key(seed), 4)
    return {
        "fourier": normal_values(streams_of[0], (2, NH, WAVES, COLS), 1.0, 6.0, ((1, 16), (3, 8))),
        "table": bell_draw_with(streams_of[1], (WAVES, NH, NDEG), (2 * NH) ** -0.5, 0.125, ((0, 8), (1, 16)), (1, 2, 16, 2.0)),
        "wavenums": draw_wavenums(jax.random.fold_in(streams_of[3], 71), 0),
    }


def one_slot(items):
    tab, sym_slot, anti_slot, mval = items
    degree = jnp.arange(NDEG, dtype=jnp.int32)
    keep = jnp.where(degree >= mval, 1.0, 0.0).astype(jnp.float32)
    even = jnp.remainder(degree - mval, 2) == 0
    band_rows = NH // N_LAT
    tab_bands = tab.astype(jnp.float32).reshape(N_LAT, band_rows, NDEG)
    sym_bands = sym_slot.reshape(N_LAT, band_rows, COLS)
    anti_bands = anti_slot.reshape(N_LAT, band_rows, COLS)
    from_sym = jnp.einsum('bjn,bjc->bnc', tab_bands, sym_bands)
    from_anti = jnp.einsum('bjn,bjc->bnc', tab_bands, anti_bands)
    chosen = jnp.where(even[None, :, None], from_sym, from_anti)
    partial_value = chosen * keep[None, :, None]
    return jnp.sum(partial_value, axis=0)


def reference(fourier, table, wavenums):
    north = fourier[0].astype(jnp.float32)
    south = fourier[1].astype(jnp.float32)
    sym = north + south
    anti = north - south
    result = lax.map(one_slot, (table, jnp.moveaxis(sym, 1, 0), jnp.moveaxis(anti, 1, 0), wavenums.astype(jnp.int32)))
    return jnp.moveaxis(result, 0, 1)
```

```python
import functools

import jax
import jax.numpy as jnp
from jax import lax
from jax.experimental import pallas as pl
from jax.experimental.pallas import tpu as pltpu
from jax.sharding import PartitionSpec as P


ROWS = 256
LANES = 256
HALF = 128
TAIL = 16
SIDE = 4
TOP = 32766.0
STEP = 64.0


def prepare_kernel(m_ref, tab_ref, out_ref, *, width, blocks):
    slot = pl.program_id(0)
    mval = m_ref[slot]
    rows = tab_ref.shape[1]
    lane = lax.broadcasted_iota(jnp.int32, (1, LANES), 1)
    out_ref[...] = jnp.zeros(out_ref.shape, out_ref.dtype)
    for d in range(blocks):
        tab = tab_ref[0, :, d * width : (d + 1) * width].astype(jnp.float32)
        offset = lane[:, :width] + (d * width) - mval
        keep = jnp.where(offset >= 0, 1.0, 0.0)
        sign = jnp.where((offset & 1) == 0, keep, -keep)
        out_ref[0, d, 0:rows, 0:width] = (tab * keep).astype(jnp.bfloat16)
        out_ref[0, d, HALF : HALF + rows, 0:width] = (tab * sign).astype(jnp.bfloat16)


def prepare(wavenums, table, blocks):
    slots, rows, degrees = table.shape
    return pl.pallas_call(
        functools.partial(prepare_kernel, width=degrees // blocks, blocks=blocks),
        grid=(slots,),
        in_specs=[
            pl.BlockSpec(memory_space=pltpu.SMEM),
            pl.BlockSpec((1, rows, degrees), lambda k: (k, 0, 0)),
        ],
        out_specs=pl.BlockSpec((1, blocks, 2 * HALF, LANES), lambda k: (k, 0, 0, 0)),
        out_shape=jax.ShapeDtypeStruct((slots, blocks, 2 * HALF, LANES), jnp.bfloat16),
        name="prepare",
    )(wavenums, table)


def own_part(four_ref, tab):
    north = four_ref[:, 0, 0].reshape(ROWS, HALF)
    south = four_ref[:, 0, 1].reshape(ROWS, HALF)
    return jnp.dot(north, tab[:HALF], preferred_element_type=jnp.float32) + jnp.dot(
        south, tab[HALF:], preferred_element_type=jnp.float32
    )


def decoded(codes, tail, row):
    at = lax.broadcasted_iota(jnp.int32, (TAIL, LANES), 0) == row
    code = jnp.sum(jnp.where(at, tail.astype(jnp.float32), 0.0), axis=0, keepdims=True)
    scale = jnp.exp2(code * (1.0 / STEP)) * (1.0 / TOP)
    return codes.astype(jnp.float32) * scale


def encode(value):
    most = jnp.maximum(jnp.max(jnp.abs(value), axis=0, keepdims=True), 1e-30)
    code = jnp.ceil(jnp.log2(most) * STEP) + 1.0
    inverse = jnp.exp2(code * (-1.0 / STEP)) * TOP
    return jnp.round(value * inverse).astype(jnp.int32).astype(jnp.int16), code


def hop_kernel(at_ref, four_ref, tab_ref, *rest, blocks, terms):
    out_ref = rest[-1]
    row = lax.broadcasted_iota(jnp.int32, (TAIL, LANES), 0)
    tail = jnp.zeros((TAIL, LANES), jnp.float32)
    for b in range(blocks):
        tab = tab_ref[(0,) + ((b, 0) if tab_ref.shape[1] > 1 else (0, b))]
        total = own_part(four_ref, tab)
        for t in range(terms):
            codes_ref, tail_ref = rest[2 * t], rest[2 * t + 1]
            which = at_ref[2] if blocks == 1 and t == 0 else b
            codes = codes_ref[b * ROWS : (b + 1) * ROWS]
            total = total + decoded(codes, tail_ref[...], which)
        codes, code = encode(total)
        out_ref[b * ROWS : (b + 1) * ROWS] = codes
        tail = jnp.where(row == b, code, tail)
    out_ref[blocks * ROWS :] = tail.astype(jnp.int32).astype(jnp.int16)


def hop(slot, at, four, tab, tab_block, tab_index, terms, blocks):
    in_specs = [
        pl.BlockSpec((8, 1, 2, 32, HALF), lambda i, at: (0, slot, 0, 0, 0)),
        pl.BlockSpec(tab_block, tab_index),
    ]
    operands = [four, tab]
    for array, held, picked in terms:
        tail_at = held * ROWS // TAIL
        if picked:
            in_specs.append(pl.BlockSpec((ROWS, LANES), lambda i, at: (at[2], 0)))
        else:
            in_specs.append(pl.BlockSpec((held * ROWS, LANES), lambda i, at: (0, 0)))
        in_specs.append(pl.BlockSpec((TAIL, LANES), lambda i, at, t=tail_at: (t, 0)))
        operands += [array, array]
    size = blocks * ROWS + TAIL
    return pl.pallas_call(
        functools.partial(hop_kernel, blocks=blocks, terms=len(terms)),
        grid_spec=pltpu.PrefetchScalarGridSpec(
            num_scalar_prefetch=1,
            grid=(1,),
            in_specs=in_specs,
            out_specs=pl.BlockSpec((size, LANES), lambda i, at: (0, 0)),
        ),
        out_shape=jax.ShapeDtypeStruct((size, LANES), jnp.int16),
        name=f"hop_{slot}",
    )(at, *operands)


def last_kernel(at_ref, four_ref, tab_ref, *rest, width):
    out_ref = rest[-1]
    slots = (len(rest) - 1) // 4
    for k in range(slots):
        first, first_tail, second, second_tail = rest[4 * k : 4 * k + 4]
        total = own_part(four_ref.at[:, k : k + 1], tab_ref[k, 0, 0])
        total = total + decoded(first[...], first_tail[...], at_ref[2 + color_is_z(k)])
        total = total + decoded(second[...], second_tail[...], 0)
        out_ref[:, k, :] = total.T[:width]


def color_is_z(slot):
    return slot % 2


def last(at, four, tab, firsts, seconds, width):
    slots = len(firsts)
    in_specs = [
        pl.BlockSpec((8, slots, 2, 32, HALF), lambda i, at: (0, 0, 0, 0, 0)),
        pl.BlockSpec((slots, 1, 1, 2 * HALF, LANES), lambda i, at: (0, at[0], at[1], 0, 0)),
    ]
    operands = [four, tab]
    for k, (first, second) in enumerate(zip(firsts, seconds)):
        place = 2 + color_is_z(k)
        in_specs += [
            pl.BlockSpec((ROWS, LANES), lambda i, at, p=place: (at[p], 0)),
            pl.BlockSpec((TAIL, LANES), lambda i, at: (SIDE * ROWS // TAIL, 0)),
            pl.BlockSpec((ROWS, LANES), lambda i, at: (0, 0)),
            pl.BlockSpec((TAIL, LANES), lambda i, at: (ROWS // TAIL, 0)),
        ]
        operands += [first, first, second, second]
    return pl.pallas_call(
        functools.partial(last_kernel, width=width),
        grid_spec=pltpu.PrefetchScalarGridSpec(
            num_scalar_prefetch=1,
            grid=(1,),
            in_specs=in_specs,
            out_specs=pl.BlockSpec((width, slots, ROWS), lambda i, at: (0, 0, 0)),
        ),
        out_shape=jax.ShapeDtypeStruct((width, slots, ROWS), jnp.float32),
        name="last",
    )(at, *operands)


def ring(axis, sign):
    pairs = []
    for x in range(SIDE):
        for z in range(SIDE):
            to = ((x + sign) % SIDE, z) if axis == 0 else (x, (z + sign) % SIDE)
            pairs.append((x * SIDE + z, to[0] * SIDE + to[1]))
    return pairs


def per_device(fourier, table, wavenums):
    slots, rows, degrees = table.shape
    lat = lax.axis_size("lat")
    width = degrees // lat
    me = lax.axis_index("lat")
    place = (me // SIDE, me % SIDE)

    split = fourier.transpose(2, 0, 3, 1)
    split = jnp.pad(split, ((0, 0), (0, 0), (0, 0), (0, HALF - rows)))
    split = split.reshape(8, slots, 2, split.shape[2], HALF)
    four = lax.all_to_all(split, "wave", split_axis=0, concat_axis=0, tiled=True)
    tab = prepare(wavenums, table, lat).reshape(slots, SIDE, SIDE, 2 * HALF, LANES)

    firsts, seconds = [None] * slots, [None] * slots
    state = [None] * slots

    def chunk_index(ring_place, sign, step):
        return (ring_place - sign * (1 + step)) % SIDE

    for step in range(SIDE - 1):
        for k in range(slots):
            axis, sign = k % 2, 1 - 2 * ((k // 2) % 2)
            chunk = chunk_index(place[axis], sign, step)
            at = jnp.stack([chunk, chunk]).astype(jnp.int32)
            if axis == 0:
                block, index = (1, 1, SIDE, 2 * HALF, LANES), lambda i, at, k=k: (k, at[0], 0, 0, 0)
            else:
                block, index = (1, SIDE, 1, 2 * HALF, LANES), lambda i, at, k=k: (k, 0, at[0], 0, 0)
            terms = [] if step == 0 else [(state[k], SIDE, False)]
            sent = hop(k, at, four, tab, block, index, terms, SIDE)
            state[k] = lax.ppermute(sent, "lat", ring(axis, sign))
    firsts = list(state)
    for step in range(SIDE - 1):
        for k in range(slots):
            axis, sign = 1 - k % 2, 1 - 2 * ((k // 2) % 2)
            chunk = chunk_index(place[axis], sign, step)
            x, z = (place[0], chunk) if axis == 1 else (chunk, place[1])
            at = jnp.stack([x, z, chunk]).astype(jnp.int32)
            block, index = (1, 1, 1, 2 * HALF, LANES), lambda i, at, k=k: (k, at[0], at[1], 0, 0)
            terms = [(firsts[k], SIDE, True)]
            if step:
                terms.append((state[k], 1, False))
            sent = hop(k, at, four, tab, block, index, terms, 1)
            state[k] = lax.ppermute(sent, "lat", ring(axis, sign))
    at = jnp.stack([place[0], place[1], place[1], place[0]]).astype(jnp.int32)
    return last(at, four, tab, firsts, state, width)


def solution(mesh):
    placed = (P(None, "lat", None, "wave"), P("wave", "lat", None), P("wave"))
    return jax.shard_map(
        per_device, mesh=mesh, in_specs=placed, out_specs=P("lat", "wave", None), check_vma=False
    )
```

```python
import functools

import jax
import jax.numpy as jnp
from jax import lax
from jax.experimental import pallas as pl
from jax.experimental.pallas import tpu as pltpu
from jax.sharding import PartitionSpec as P


ROWS = 256
LANES = 256
HALF = 128
TAIL = 16
SIDE = 4
PAIR = 2
TOP = 32766.0
STEP = 64.0


def prepare_kernel(m_ref, tab_ref, out_ref, *, width, blocks):
    slot = pl.program_id(0)
    mval = m_ref[slot]
    rows, degrees = tab_ref.shape[1:]
    lane = lax.broadcasted_iota(jnp.int32, (1, LANES), 1)
    for d in range(blocks):
        held = min(LANES, degrees - d * width)
        tab = tab_ref[0, :, d * width : d * width + held]
        if held < LANES:
            tab = jnp.concatenate([tab, jnp.zeros((rows, LANES - held), tab.dtype)], axis=1)
        tab = jnp.concatenate([tab, jnp.zeros((HALF - rows, LANES), tab.dtype)], axis=0)
        offset = lane + (d * width) - mval
        keep = jnp.where(offset >= 0, 1.0, 0.0)
        sign = jnp.where((offset & 1) == 0, keep, -keep)
        out_ref[0, d, :HALF] = tab * keep.astype(jnp.bfloat16)
        out_ref[0, d, HALF:] = tab * sign.astype(jnp.bfloat16)


def prepare(wavenums, table, blocks):
    slots, rows, degrees = table.shape
    return pl.pallas_call(
        functools.partial(prepare_kernel, width=degrees // blocks, blocks=blocks),
        grid=(slots,),
        in_specs=[
            pl.BlockSpec(memory_space=pltpu.SMEM),
            pl.BlockSpec((1, rows, degrees), lambda k: (k, 0, 0)),
        ],
        out_specs=pl.BlockSpec((1, blocks, 2 * HALF, LANES), lambda k: (k, 0, 0, 0)),
        out_shape=jax.ShapeDtypeStruct((slots, blocks, 2 * HALF, LANES), jnp.bfloat16),
        compiler_params=pltpu.CompilerParams(vmem_limit_bytes=16 << 20),
        name="prepare",
    )(wavenums, table)


def own_part(four_ref, slot, tab):
    north = four_ref[:, slot, 0].reshape(ROWS, HALF)
    south = four_ref[:, slot, 1].reshape(ROWS, HALF)
    return jnp.dot(north, tab[:HALF], preferred_element_type=jnp.float32) + jnp.dot(
        south, tab[HALF:], preferred_element_type=jnp.float32
    )


def decoded(codes, tail, row):
    at = lax.broadcasted_iota(jnp.int32, (TAIL, LANES), 0) == row
    code = jnp.sum(jnp.where(at, tail.astype(jnp.float32), 0.0), axis=0, keepdims=True)
    scale = jnp.exp2(code * (1.0 / STEP)) * (1.0 / TOP)
    return codes.astype(jnp.float32) * scale


def encode(value):
    most = jnp.maximum(jnp.max(jnp.abs(value), axis=0, keepdims=True), 1e-30)
    code = jnp.ceil(jnp.log2(most) * STEP) + 1.0
    inverse = jnp.exp2(code * (-1.0 / STEP)) * TOP
    return jnp.round(value * inverse).astype(jnp.int32).astype(jnp.int16), code


def store_coded(out_ref, values):
    row = lax.broadcasted_iota(jnp.int32, (TAIL, LANES), 0)
    tail = jnp.zeros((TAIL, LANES), jnp.float32)
    count = 0
    for value in values:
        codes, code = encode(value)
        out_ref[count * ROWS : (count + 1) * ROWS] = codes
        tail = jnp.where(row == count, code, tail)
        count += 1
    out_ref[count * ROWS :] = tail.astype(jnp.int32).astype(jnp.int16)


def ring_kernel(at_ref, four_ref, tab_ref, *rest, across):
    out_ref = rest[-1]

    def values():
        for slot in range(PAIR):
            for b in range(SIDE):
                total = own_part(four_ref, slot, tab_ref[slot, 0, b] if across else tab_ref[slot, b, 0])
                if len(rest) > 1:
                    at = slot * SIDE + b
                    total = total + decoded(rest[0][at * ROWS : (at + 1) * ROWS], rest[0][PAIR * SIDE * ROWS :], at)
                yield total

    store_coded(out_ref, values())


def moving(at, axis, sign, step):
    return (at[axis] - sign * (1 + step)) & (SIDE - 1)


def second_kernel(at_ref, four_ref, tab_ref, *rest, hop):
    out_ref = rest[-1]
    first_tail = rest[PAIR]
    block = moving(at_ref, *hop)

    def values():
        for slot in range(PAIR):
            total = own_part(four_ref, slot, tab_ref[slot, 0, 0])
            total = total + decoded(rest[slot][...], first_tail[...], slot * SIDE + block)
            if len(rest) > PAIR + 2:
                state = rest[PAIR + 1]
                total = total + decoded(state[slot * ROWS : (slot + 1) * ROWS], state[PAIR * ROWS :], slot)
            yield total

    store_coded(out_ref, values())


def first_specs(hop):
    specs = []
    for slot in range(PAIR):
        specs.append(pl.BlockSpec((ROWS, LANES), lambda i, at, s=slot: (s * SIDE + moving(at, *hop), 0)))
    specs.append(pl.BlockSpec((TAIL, LANES), lambda i, at: (PAIR * SIDE * ROWS // TAIL, 0)))
    return specs


def call(body, name, at, operands, in_specs, rows):
    return pl.pallas_call(
        body,
        grid_spec=pltpu.PrefetchScalarGridSpec(
            num_scalar_prefetch=1,
            grid=(1,),
            in_specs=in_specs,
            out_specs=pl.BlockSpec((rows, LANES), lambda i, at: (0, 0)),
        ),
        out_shape=jax.ShapeDtypeStruct((rows, LANES), jnp.int16),
        compiler_params=pltpu.CompilerParams(vmem_limit_bytes=16 << 20),
        name=name,
    )(at, *operands)


def whole(array):
    return pl.BlockSpec(array.shape, lambda i, at: (0,) * array.ndim)


def four_of(color):
    return pl.BlockSpec((8, PAIR, 2, 32, HALF), lambda i, at: (0, color, 0, 0, 0))


def first_hop(color, at, hop, four, tab, state):
    across = hop[0] == 0
    if across:
        spec = pl.BlockSpec((PAIR, 1, SIDE, 2 * HALF, LANES), lambda i, at: (color, moving(at, *hop), 0, 0, 0))
    else:
        spec = pl.BlockSpec((PAIR, SIDE, 1, 2 * HALF, LANES), lambda i, at: (color, 0, moving(at, *hop), 0, 0))
    body = functools.partial(ring_kernel, across=across)
    operands, specs = [four, tab], [four_of(color), spec]
    if state is not None:
        operands.append(state)
        specs.append(whole(state))
    return call(body, "first", at, operands, specs, PAIR * SIDE * ROWS + TAIL)


def second_hop(color, at, hop, four, tab, first, state):
    def index(i, at):
        if hop[0] == 0:
            return color, moving(at, *hop), at[1], 0, 0
        return color, at[0], moving(at, *hop), 0, 0

    spec = pl.BlockSpec((PAIR, 1, 1, 2 * HALF, LANES), index)
    operands = [four, tab] + [first] * (PAIR + 1)
    specs = [four_of(color), spec] + first_specs(hop)
    if state is not None:
        operands.append(state)
        specs.append(whole(state))
    return call(functools.partial(second_kernel, hop=hop), "second", at, operands, specs, PAIR * ROWS + TAIL)


def last_kernel(at_ref, four_ref, tab_ref, *rest, width, hops):
    out_ref = rest[-1]
    per = PAIR + 2
    for color, hop in enumerate(hops):
        mine = rest[color * per : (color + 1) * per]
        for slot in range(PAIR):
            k = color * PAIR + slot
            total = own_part(four_ref, k, tab_ref[k, 0, 0])
            total = total + decoded(mine[slot][...], mine[PAIR][...], slot * SIDE + moving(at_ref, *hop))
            state = mine[PAIR + 1]
            total = total + decoded(state[slot * ROWS : (slot + 1) * ROWS], state[PAIR * ROWS :], slot)
            out_ref[:, k, :] = total.T[:width]


def last(at, hops, four, tab, firsts, states, width):
    slots = tab.shape[0]
    in_specs = [
        whole(four),
        pl.BlockSpec((slots, 1, 1, 2 * HALF, LANES), lambda i, at: (0, at[0], at[1], 0, 0)),
    ]
    operands = [four, tab]
    for hop, first, state in zip(hops, firsts, states):
        in_specs += first_specs(hop) + [whole(state)]
        operands += [first] * (PAIR + 1) + [state]
    return pl.pallas_call(
        functools.partial(last_kernel, width=width, hops=hops),
        grid_spec=pltpu.PrefetchScalarGridSpec(
            num_scalar_prefetch=1,
            grid=(1,),
            in_specs=in_specs,
            out_specs=pl.BlockSpec((width, slots, ROWS), lambda i, at: (0, 0, 0)),
        ),
        out_shape=jax.ShapeDtypeStruct((width, slots, ROWS), jnp.float32),
        compiler_params=pltpu.CompilerParams(vmem_limit_bytes=32 << 20),
        name="last",
    )(at, *operands)


def ring(axis, sign):
    pairs = []
    for x in range(SIDE):
        for z in range(SIDE):
            to = ((x + sign) % SIDE, z) if axis == 0 else (x, (z + sign) % SIDE)
            pairs.append((x * SIDE + z, to[0] * SIDE + to[1]))
    return pairs


def per_device(fourier, table, wavenums):
    slots, rows, degrees = table.shape
    lat = lax.axis_size("lat")
    width = degrees // lat
    me = lax.axis_index("lat")

    split = fourier.transpose(2, 0, 3, 1)
    split = jnp.pad(split, ((0, 0), (0, 0), (0, 0), (0, HALF - rows)))
    split = split.reshape(8, slots, 2, split.shape[2], HALF)
    four = lax.all_to_all(split, "wave", split_axis=0, concat_axis=0, tiled=True)
    tab = prepare(wavenums, table, lat).reshape(slots, SIDE, SIDE, 2 * HALF, LANES)

    at = jnp.stack([me // SIDE, me % SIDE]).astype(jnp.int32)
    colors = [(0, 1), (1, 1), (0, -1), (1, -1)]
    states = [None] * len(colors)
    for step in range(SIDE - 1):
        for color, (axis, sign) in enumerate(colors):
            sent = first_hop(color, at, (axis, sign, step), four, tab, states[color])
            states[color] = lax.ppermute(sent, "lat", ring(axis, sign))
    firsts, states = states, [None] * len(colors)
    for step in range(SIDE - 1):
        for color, (axis, sign) in enumerate(colors):
            sent = second_hop(color, at, (1 - axis, sign, step), four, tab, firsts[color], states[color])
            states[color] = lax.ppermute(sent, "lat", ring(1 - axis, sign))
    hops = [(1 - axis, sign, SIDE - 1) for axis, sign in colors]
    return last(at, hops, four, tab, firsts, states, width)


def solution(mesh):
    placed = (P(None, "lat", None, "wave"), P("wave", "lat", None), P("wave"))
    return jax.shard_map(
        per_device, mesh=mesh, in_specs=placed, out_specs=P("lat", "wave", None), check_vma=False
    )
```

```python
import functools

import jax
import jax.numpy as jnp
from jax import lax
from jax.experimental import pallas as pl
from jax.experimental.pallas import tpu as pltpu
from jax.sharding import PartitionSpec as P


ROWS = 256
LANES = 256
HALF = 128
TILE = 128
TILES = 3
TAIL = 16
SIDE = 4
PAIR = 2
TOP = 32766.0
STEP = 64.0


def own_part(four_ref, slot, tiles, first, mval):
    tab = jnp.concatenate([tile[slot] for tile in tiles], axis=1).astype(jnp.float32)
    shift = first & (TILE - 1)
    tab = pltpu.roll(tab, TILES * TILE - shift, 1)[:, :LANES]
    tab = jnp.concatenate([tab, jnp.zeros((HALF - tab.shape[0], LANES), tab.dtype)], axis=0)
    offset = lax.broadcasted_iota(jnp.int32, (1, LANES), 1) + first - mval
    keep = jnp.where(offset >= 0, 1.0, 0.0)
    sign = jnp.where((offset & 1) == 0, keep, -keep)
    tab = jnp.concatenate([(tab * keep).astype(jnp.bfloat16), (tab * sign).astype(jnp.bfloat16)], axis=0)
    north = four_ref[:, slot, 0].reshape(ROWS, HALF)
    south = four_ref[:, slot, 1].reshape(ROWS, HALF)
    return jnp.dot(north, tab[:HALF], preferred_element_type=jnp.float32) + jnp.dot(
        south, tab[HALF:], preferred_element_type=jnp.float32
    )


def decoded(codes, tail, row):
    at = lax.broadcasted_iota(jnp.int32, (TAIL, LANES), 0) == row
    code = jnp.sum(jnp.where(at, tail.astype(jnp.float32), 0.0), axis=0, keepdims=True)
    scale = jnp.exp2(code * (1.0 / STEP)) * (1.0 / TOP)
    return codes.astype(jnp.float32) * scale


def encode(value):
    most = jnp.maximum(jnp.max(jnp.abs(value), axis=0, keepdims=True), 1e-30)
    code = jnp.ceil(jnp.log2(most) * STEP) + 1.0
    inverse = jnp.exp2(code * (-1.0 / STEP)) * TOP
    return jnp.round(value * inverse).astype(jnp.int32).astype(jnp.int16), code


def store_coded(out_ref, values):
    row = lax.broadcasted_iota(jnp.int32, (TAIL, LANES), 0)
    tail = jnp.zeros((TAIL, LANES), jnp.float32)
    count = 0
    for value in values:
        codes, code = encode(value)
        out_ref[count * ROWS : (count + 1) * ROWS] = codes
        tail = jnp.where(row == count, code, tail)
        count += 1
    out_ref[count * ROWS :] = tail.astype(jnp.int32).astype(jnp.int16)


def moving(at, axis, sign, step):
    return (at[axis] - sign * (1 + step)) & (SIDE - 1)


def block_at(at, hop, b):
    if b is None:
        return moving(at, *hop) * SIDE + at[1] if hop[0] == 0 else at[0] * SIDE + moving(at, *hop)
    return moving(at, *hop) * SIDE + b if hop[0] == 0 else b * SIDE + moving(at, *hop)


def tile_specs(slots, rows, width, group, blocks):
    specs = []
    for block in blocks:
        for t in range(TILES):

            def index(i, at, block=block, t=t):
                return group, 0, block(at) * width // TILE + t

            specs.append(pl.BlockSpec((slots, rows, TILE), index))
    return specs


def ring_kernel(at_ref, four_ref, *rest, hop, group, width):
    out_ref = rest[-1]
    tiles, state = rest[: SIDE * TILES], rest[SIDE * TILES : -1]

    def values():
        for slot in range(PAIR):
            mval = at_ref[2 + group * PAIR + slot]
            for b in range(SIDE):
                first = block_at(at_ref, hop, b) * width
                total = own_part(four_ref, slot, tiles[b * TILES : (b + 1) * TILES], first, mval)
                if state:
                    at = slot * SIDE + b
                    total = total + decoded(state[0][at * ROWS : (at + 1) * ROWS], state[0][PAIR * SIDE * ROWS :], at)
                yield total

    store_coded(out_ref, values())


def second_kernel(at_ref, four_ref, *rest, hop, group, width):
    out_ref = rest[-1]
    tiles, firsts, state = rest[:TILES], rest[TILES : TILES + PAIR + 1], rest[TILES + PAIR + 1 : -1]
    first = block_at(at_ref, hop, None) * width

    def values():
        for slot in range(PAIR):
            total = own_part(four_ref, slot, tiles, first, at_ref[2 + group * PAIR + slot])
            total = total + decoded(firsts[slot][...], firsts[PAIR][...], slot * SIDE + moving(at_ref, *hop))
            if state:
                total = total + decoded(state[0][slot * ROWS : (slot + 1) * ROWS], state[0][PAIR * ROWS :], slot)
            yield total

    store_coded(out_ref, values())


def first_specs(hop):
    specs = []
    for slot in range(PAIR):
        specs.append(pl.BlockSpec((ROWS, LANES), lambda i, at, s=slot: (s * SIDE + moving(at, *hop), 0)))
    specs.append(pl.BlockSpec((TAIL, LANES), lambda i, at: (PAIR * SIDE * ROWS // TAIL, 0)))
    return specs


def call(body, name, at, operands, in_specs, rows):
    return pl.pallas_call(
        body,
        grid_spec=pltpu.PrefetchScalarGridSpec(
            num_scalar_prefetch=1,
            grid=(1,),
            in_specs=in_specs,
            out_specs=pl.BlockSpec((rows, LANES), lambda i, at: (0, 0)),
        ),
        out_shape=jax.ShapeDtypeStruct((rows, LANES), jnp.int16),
        compiler_params=pltpu.CompilerParams(vmem_limit_bytes=16 << 20),
        name=name,
    )(at, *operands)


def whole(array):
    return pl.BlockSpec(array.shape, lambda i, at: (0,) * array.ndim)


def four_of(group):
    return pl.BlockSpec((8, PAIR, 2, 32, HALF), lambda i, at: (0, group, 0, 0, 0))


def first_hop(group, at, hop, four, tab, state, width):
    blocks = [functools.partial(block_at, hop=hop, b=b) for b in range(SIDE)]
    specs = [four_of(group)] + tile_specs(PAIR, tab.shape[1], width, group, blocks)
    operands = [four] + [tab] * (SIDE * TILES)
    if state is not None:
        operands.append(state)
        specs.append(whole(state))
    body = functools.partial(ring_kernel, hop=hop, group=group, width=width)
    return call(body, "first", at, operands, specs, PAIR * SIDE * ROWS + TAIL)


def second_hop(group, at, hop, four, tab, first, state, width):
    blocks = [functools.partial(block_at, hop=hop, b=None)]
    specs = [four_of(group)] + tile_specs(PAIR, tab.shape[1], width, group, blocks) + first_specs(hop)
    operands = [four] + [tab] * TILES + [first] * (PAIR + 1)
    if state is not None:
        operands.append(state)
        specs.append(whole(state))
    body = functools.partial(second_kernel, hop=hop, group=group, width=width)
    return call(body, "second", at, operands, specs, PAIR * ROWS + TAIL)


def last_kernel(at_ref, four_ref, *rest, width, hops):
    out_ref = rest[-1]
    tiles, rest = rest[:TILES], rest[TILES:]
    per = PAIR + 2
    for group, hop in enumerate(hops):
        mine = rest[group * per : (group + 1) * per]
        for slot in range(PAIR):
            k = group * PAIR + slot
            total = own_part(four_ref, k, tiles, (at_ref[0] * SIDE + at_ref[1]) * width, at_ref[2 + k])
            total = total + decoded(mine[slot][...], mine[PAIR][...], slot * SIDE + moving(at_ref, *hop))
            state = mine[PAIR + 1]
            total = total + decoded(state[slot * ROWS : (slot + 1) * ROWS], state[PAIR * ROWS :], slot)
            out_ref[:, k, :] = total.T[:width]


def last(at, hops, four, tab, firsts, states, width):
    slots, rows = tab.shape[:2]
    in_specs = [whole(four)] + tile_specs(slots, rows, width, 0, [lambda at: at[0] * SIDE + at[1]])
    operands = [four] + [tab] * TILES
    for hop, first, state in zip(hops, firsts, states):
        in_specs += first_specs(hop) + [whole(state)]
        operands += [first] * (PAIR + 1) + [state]
    return pl.pallas_call(
        functools.partial(last_kernel, width=width, hops=hops),
        grid_spec=pltpu.PrefetchScalarGridSpec(
            num_scalar_prefetch=1,
            grid=(1,),
            in_specs=in_specs,
            out_specs=pl.BlockSpec((width, slots, ROWS), lambda i, at: (0, 0, 0)),
        ),
        out_shape=jax.ShapeDtypeStruct((width, slots, ROWS), jnp.float32),
        compiler_params=pltpu.CompilerParams(vmem_limit_bytes=32 << 20),
        name="last",
    )(at, *operands)


def ring(axis, sign):
    pairs = []
    for x in range(SIDE):
        for z in range(SIDE):
            to = ((x + sign) % SIDE, z) if axis == 0 else (x, (z + sign) % SIDE)
            pairs.append((x * SIDE + z, to[0] * SIDE + to[1]))
    return pairs


def per_device(fourier, table, wavenums):
    slots, rows, degrees = table.shape
    lat = lax.axis_size("lat")
    width = degrees // lat
    me = lax.axis_index("lat")

    split = fourier.transpose(2, 0, 3, 1)
    split = jnp.pad(split, ((0, 0), (0, 0), (0, 0), (0, HALF - rows)))
    split = split.reshape(8, slots, 2, split.shape[2], HALF)
    four = lax.all_to_all(split, "wave", split_axis=0, concat_axis=0, tiled=True)
    at = jnp.concatenate([jnp.stack([me // SIDE, me % SIDE]).astype(jnp.int32), wavenums])
    groups = [(0, 1), (1, 1), (0, -1), (1, -1)]

    states = [None] * len(groups)
    for step in range(SIDE - 1):
        for group, (axis, sign) in enumerate(groups):
            sent = first_hop(group, at, (axis, sign, step), four, table, states[group], width)
            states[group] = lax.ppermute(sent, "lat", ring(axis, sign))
    firsts, states = states, [None] * len(groups)
    for step in range(SIDE - 1):
        for group, (axis, sign) in enumerate(groups):
            hop = (1 - axis, sign, step)
            sent = second_hop(group, at, hop, four, table, firsts[group], states[group], width)
            states[group] = lax.ppermute(sent, "lat", ring(1 - axis, sign))
    hops = [(1 - axis, sign, SIDE - 1) for axis, sign in groups]
    return last(at, hops, four, table, firsts, states, width)


def solution(mesh):
    placed = (P(None, "lat", None, "wave"), P("wave", "lat", None), P("wave"))
    return jax.shard_map(
        per_device, mesh=mesh, in_specs=placed, out_specs=P("lat", "wave", None), check_vma=False
    )
```

```python
import functools

import jax
import jax.numpy as jnp
from jax import lax
from jax.experimental import pallas as pl
from jax.experimental.pallas import tpu as pltpu
from jax.sharding import PartitionSpec as P


ROWS = 256
LANES = 256
HALF = 128
TILE = 128
TILES = 3
TAIL = 16
SIDE = 4
PAIR = 2
GROUPS = 4
TOP = 32766.0
STEP = 64.0


def own_part(four_ref, slot, tiles, row, first, mval):
    tab = jnp.concatenate([tile[row] for tile in tiles], axis=1).astype(jnp.float32)
    shift = first & (TILE - 1)
    tab = pltpu.roll(tab, TILES * TILE - shift, 1)[:, :LANES]
    tab = jnp.concatenate([tab, jnp.zeros((HALF - tab.shape[0], LANES), tab.dtype)], axis=0)
    offset = lax.broadcasted_iota(jnp.int32, (1, LANES), 1) + first - mval
    keep = jnp.where(offset >= 0, 1.0, 0.0)
    sign = jnp.where((offset & 1) == 0, keep, -keep)
    tab = jnp.concatenate([(tab * keep).astype(jnp.bfloat16), (tab * sign).astype(jnp.bfloat16)], axis=0)
    north = four_ref[:, slot, 0].reshape(ROWS, HALF)
    south = four_ref[:, slot, 1].reshape(ROWS, HALF)
    return jnp.dot(north, tab[:HALF], preferred_element_type=jnp.float32) + jnp.dot(
        south, tab[HALF:], preferred_element_type=jnp.float32
    )


def decoded(codes, tail, row):
    at = lax.broadcasted_iota(jnp.int32, (TAIL, LANES), 0) == row
    code = jnp.sum(jnp.where(at, tail.astype(jnp.float32), 0.0), axis=0, keepdims=True)
    scale = jnp.exp2(code * (1.0 / STEP)) * (1.0 / TOP)
    return codes.astype(jnp.float32) * scale


def encode(value):
    most = jnp.maximum(jnp.max(jnp.abs(value), axis=0, keepdims=True), 1e-30)
    code = jnp.ceil(jnp.log2(most) * STEP) + 1.0
    inverse = jnp.exp2(code * (-1.0 / STEP)) * TOP
    return jnp.round(value * inverse).astype(jnp.int32).astype(jnp.int16), code


def store_coded(out_ref, values):
    row = lax.broadcasted_iota(jnp.int32, (TAIL, LANES), 0)
    tail = jnp.zeros((TAIL, LANES), jnp.float32)
    count = 0
    for value in values:
        codes, code = encode(value)
        out_ref[count * ROWS : (count + 1) * ROWS] = codes
        tail = jnp.where(row == count, code, tail)
        count += 1
    out_ref[count * ROWS :] = tail.astype(jnp.int32).astype(jnp.int16)


def chunk_at(at, axis, ahead):
    return (at[axis] + ahead) & (SIDE - 1)


def block_at(at, axis, ahead, b):
    chunk = chunk_at(at, axis, ahead)
    other = at[1 - axis] if b is None else b
    return chunk * SIDE + other if axis == 0 else other * SIDE + chunk


def tile_specs(slots, rows, width, group, blocks):
    specs = []
    for block in blocks:
        for t in range(TILES):

            def index(i, at, block=block, t=t):
                return group, 0, block(at) * width // TILE + t

            specs.append(pl.BlockSpec((slots, rows, TILE), index))
    return specs


def first_kernel(at_ref, four_ref, *rest, axis, ahead, group, width, terms):
    out_ref = rest[-1]
    tiles, states = rest[: SIDE * TILES], rest[SIDE * TILES : SIDE * TILES + terms]

    def values():
        for slot in range(PAIR):
            mval = at_ref[2 + group * PAIR + slot]
            for b in range(SIDE):
                first = block_at(at_ref, axis, ahead, b) * width
                total = own_part(four_ref, slot, tiles[b * TILES : (b + 1) * TILES], slot, first, mval)
                at = slot * SIDE + b
                for state in states:
                    total = total + decoded(state[at * ROWS : (at + 1) * ROWS], state[PAIR * SIDE * ROWS :], at)
                yield total

    store_coded(out_ref, values())


def summed(at_ref, four_ref, place, slot, mval, refs, axis, ahead, width):
    first = block_at(at_ref, axis, ahead, None) * width
    total = own_part(four_ref, place, refs[:TILES], slot, first, mval)
    refs = refs[TILES:]
    for _ in range(2):
        total = total + decoded(refs[slot][...], refs[PAIR][...], slot * SIDE + chunk_at(at_ref, axis, ahead))
        refs = refs[PAIR + 1 :]
    for state in refs:
        total = total + decoded(state[slot * ROWS : (slot + 1) * ROWS], state[PAIR * ROWS :], slot)
    return total


def second_kernel(at_ref, four_ref, *rest, axis, aheads, width, terms):
    per = TILES + 2 * (PAIR + 1) + terms
    for pair, ahead in enumerate(aheads):
        refs = rest[pair * per : (pair + 1) * per]

        def values():
            for slot in range(PAIR):
                at = pair * PAIR + slot
                mval = at_ref[2 + (1 - axis) * 2 * PAIR + at]
                yield summed(at_ref, four_ref, at, slot, mval, refs, axis, ahead, width)

        store_coded(rest[pair - 2], values())


def last_kernel(at_ref, four_ref, *rest, width):
    out_ref = rest[-1]
    per = TILES + 2 * (PAIR + 1) + 2
    for group in range(GROUPS):
        refs = rest[group * per : (group + 1) * per]
        for slot in range(PAIR):
            k = group * PAIR + slot
            total = summed(at_ref, four_ref, k, slot, at_ref[2 + k], refs, 1 - group // 2, 0, width)
            out_ref[:, k, :] = total.T[:width]


def whole(array):
    return pl.BlockSpec(array.shape, lambda i, at: (0,) * array.ndim)


def four_of(slots, index):
    return pl.BlockSpec((8, slots, 2, 32, HALF), lambda i, at: (0, index, 0, 0, 0))


def second_operands(group, axis, ahead, tab, firsts, states, width):
    blocks = [functools.partial(block_at, axis=axis, ahead=ahead, b=None)]
    specs = tile_specs(PAIR, tab.shape[1], width, group, blocks)
    operands = [tab] * TILES
    for first in firsts:
        for slot in range(PAIR):
            specs.append(pl.BlockSpec((ROWS, LANES), lambda i, at, s=slot: (s * SIDE + chunk_at(at, axis, ahead), 0)))
        specs.append(pl.BlockSpec((TAIL, LANES), lambda i, at: (PAIR * SIDE * ROWS // TAIL, 0)))
        operands += [first] * (PAIR + 1)
    return specs + [whole(state) for state in states], operands + list(states)


def call(body, at, operands, in_specs, out_shapes, limit=10):
    outs = [jax.ShapeDtypeStruct(shape, dtype) for shape, dtype in out_shapes]
    return pl.pallas_call(
        body,
        grid_spec=pltpu.PrefetchScalarGridSpec(
            num_scalar_prefetch=1, grid=(1,), in_specs=in_specs, out_specs=[whole(out) for out in outs]
        ),
        out_shape=outs,
        compiler_params=pltpu.CompilerParams(vmem_limit_bytes=limit << 20),
    )(at, *operands)


def first_hop(group, ahead, at, four, tab, states, width):
    axis = group // 2
    blocks = [functools.partial(block_at, axis=axis, ahead=ahead, b=b) for b in range(SIDE)]
    specs = [four_of(PAIR, group)] + tile_specs(PAIR, tab.shape[1], width, group, blocks)
    specs += [whole(state) for state in states]
    operands = [four] + [tab] * (SIDE * TILES) + list(states)
    body = functools.partial(
        first_kernel, axis=axis, ahead=ahead, group=group, width=width, terms=len(states)
    )
    out = ((PAIR * SIDE * ROWS + TAIL, LANES), jnp.int16)
    return call(body, at, operands, specs, [out])[0]


def second_hop(start, aheads, at, four, tab, firsts, states, width):
    axis = 1 - start // 2
    specs, operands = [four_of(2 * PAIR, start // 2)], [four]
    for pair, ahead in enumerate(aheads):
        more, arrays = second_operands(start + pair, axis, ahead, tab, firsts[pair], states[pair], width)
        specs, operands = specs + more, operands + arrays
    body = functools.partial(second_kernel, axis=axis, aheads=aheads, width=width, terms=len(states[0]))
    return call(body, at, operands, specs, [((PAIR * ROWS + TAIL, LANES), jnp.int16)] * 2)


def last(at, four, tab, firsts, states, width):
    specs, operands = [whole(four)], [four]
    for group in range(GROUPS):
        more, arrays = second_operands(group, 1 - group // 2, 0, tab, firsts[group], states[group], width)
        specs, operands = specs + more, operands + arrays
    out = ((width, tab.shape[0], ROWS), jnp.float32)
    return call(functools.partial(last_kernel, width=width), at, operands, specs, [out], 24)[0]


def ring(axis, sign):
    pairs = []
    for x in range(SIDE):
        for z in range(SIDE):
            to = ((x + sign) % SIDE, z) if axis == 0 else (x, (z + sign) % SIDE)
            pairs.append((x * SIDE + z, to[0] * SIDE + to[1]))
    return pairs


def per_device(fourier, table, wavenums):
    slots, rows, degrees = table.shape
    lat = lax.axis_size("lat")
    width = degrees // lat
    me = lax.axis_index("lat")

    split = fourier.transpose(2, 0, 3, 1)
    split = jnp.pad(split, ((0, 0), (0, 0), (0, 0), (0, HALF - rows)))
    split = split.reshape(8, slots, 2, split.shape[2], HALF)
    four = lax.all_to_all(split, "wave", split_axis=0, concat_axis=0, tiled=True)
    at = jnp.concatenate([jnp.stack([me // SIDE, me % SIDE]).astype(jnp.int32), wavenums])

    def send(array, axis, sign):
        return lax.ppermute(array, "lat", ring(axis, sign))

    def first(group, ahead, states):
        return first_hop(group, ahead, at, four, table, states, width)

    def second(start, aheads, firsts, states):
        return second_hop(start, aheads, at, four, table, firsts, states, width)

    ways = [1 - 2 * (group % 2) for group in range(GROUPS)]
    every = range(GROUPS)
    far = [first(g, 2, []) for g in every]
    got_far = [send(far[g], g // 2, ways[g]) for g in every]
    near = [first(g, -ways[g], []) for g in every]
    got_near = [send(near[g], g // 2, -ways[g]) for g in every]
    both = [first(g, ways[g], [got_far[g]]) for g in every]
    got_both = [send(both[g], g // 2, ways[g]) for g in every]
    firsts = list(zip(got_near, got_both))

    halves = [(0, 1), (2, 3)]
    of = [(firsts[p], firsts[q]) for p, q in halves]
    far = [second(2 * h, (2, 2), of[h], ((), ())) for h in range(2)]
    got_far = [send(far[g // 2][g % 2], 1 - g // 2, ways[g]) for g in every]
    near = [second(2 * h, (-1, 1), of[h], ((), ())) for h in range(2)]
    got_near = [send(near[g // 2][g % 2], 1 - g // 2, -ways[g]) for g in every]
    both = [second(2 * h, (1, -1), of[h], ((got_far[p],), (got_far[q],))) for h, (p, q) in enumerate(halves)]
    got_both = [send(both[g // 2][g % 2], 1 - g // 2, ways[g]) for g in every]
    return last(at, four, table, firsts, list(zip(got_near, got_both)), width)


def solution(mesh):
    placed = (P(None, "lat", None, "wave"), P("wave", "lat", None), P("wave"))
    return jax.shard_map(
        per_device, mesh=mesh, in_specs=placed, out_specs=P("lat", "wave", None), check_vma=False
    )
```

```python
import functools

import jax
import jax.numpy as jnp
from jax import lax
from jax.experimental import pallas as pl
from jax.experimental.layout import Layout, with_layout_constraint
from jax.experimental.pallas import tpu as pltpu
from jax.sharding import PartitionSpec as P


ROWS = 256
LANES = 256
HALF = 128
TILE = 128
TILES = 3
TAIL = 16
SIDE = 4
PAIR = 2
GROUPS = 4
TOP = 32766.0
STEP = 64.0


def own_part(four_ref, slot, tiles, row, first, mval):
    tab = jnp.concatenate([tile[row] for tile in tiles], axis=1).astype(jnp.float32)
    shift = first & (TILE - 1)
    tab = pltpu.roll(tab, TILES * TILE - shift, 1)[:, :LANES]
    tab = jnp.concatenate([tab, jnp.zeros((HALF - tab.shape[0], LANES), tab.dtype)], axis=0)
    offset = lax.broadcasted_iota(jnp.int32, (1, LANES), 1) + first - mval
    keep = jnp.where(offset >= 0, 1.0, 0.0)
    sign = jnp.where((offset & 1) == 0, keep, -keep)
    tab = jnp.concatenate([(tab * keep).astype(jnp.bfloat16), (tab * sign).astype(jnp.bfloat16)], axis=0)
    north = four_ref[:, slot, 0].reshape(ROWS, HALF)
    south = four_ref[:, slot, 1].reshape(ROWS, HALF)
    return jnp.dot(north, tab[:HALF], preferred_element_type=jnp.float32) + jnp.dot(
        south, tab[HALF:], preferred_element_type=jnp.float32
    )


def decoded(codes, tail, row):
    at = lax.broadcasted_iota(jnp.int32, (TAIL, LANES), 0) == row
    code = jnp.sum(jnp.where(at, tail.astype(jnp.float32), 0.0), axis=0, keepdims=True)
    scale = jnp.exp2(code * (1.0 / STEP)) * (1.0 / TOP)
    return codes.astype(jnp.float32) * scale


def encode(value):
    most = jnp.maximum(jnp.max(jnp.abs(value), axis=0, keepdims=True), 1e-30)
    code = jnp.ceil(jnp.log2(most) * STEP) + 1.0
    inverse = jnp.exp2(code * (-1.0 / STEP)) * TOP
    return jnp.round(value * inverse).astype(jnp.int32).astype(jnp.int16), code


def rows_at(at):
    return pl.ds(at * ROWS if isinstance(at, int) else pl.multiple_of(at * ROWS, ROWS), ROWS)


def store_coded(out_ref, blocks, value, loop):
    row = lax.broadcasted_iota(jnp.int32, (TAIL, LANES), 0)

    def one(slot, tail):
        for b in range(blocks):
            at = slot * blocks + b
            codes, code = encode(value(slot, b))
            out_ref[rows_at(at)] = codes
            tail = jnp.where(row == at, code, tail)
        return tail

    tail = jnp.zeros((TAIL, LANES), jnp.float32)
    if loop:
        tail = lax.fori_loop(0, PAIR, one, tail)
    else:
        for slot in range(PAIR):
            tail = one(slot, tail)
    out_ref[PAIR * blocks * ROWS :] = tail.astype(jnp.int32).astype(jnp.int16)


def chunk_at(at, axis, ahead):
    return (at[axis] + ahead) & (SIDE - 1)


def block_at(at, axis, ahead, b):
    chunk = chunk_at(at, axis, ahead)
    other = at[1 - axis] if b is None else b
    return chunk * SIDE + other if axis == 0 else other * SIDE + chunk


def tile_specs(slots, rows, width, group, blocks):
    specs = []
    for block in blocks:
        for t in range(TILES):

            def index(i, at, block=block, t=t):
                return group, 0, block(at) * width // TILE + t

            specs.append(pl.BlockSpec((slots, rows, TILE), index))
    return specs


def first_kernel(at_ref, four_ref, *rest, axis, ahead, group, width, terms):
    out_ref = rest[-1]
    tiles, states = rest[: SIDE * TILES], rest[SIDE * TILES : SIDE * TILES + terms]

    def value(slot, b):
        first = block_at(at_ref, axis, ahead, b) * width
        mval = at_ref[2 + group * PAIR + slot]
        total = own_part(four_ref, slot, tiles[b * TILES : (b + 1) * TILES], slot, first, mval)
        at = slot * SIDE + b
        for state in states:
            total = total + decoded(rows_of(state, at), state[PAIR * SIDE * ROWS :], at)
        return total

    store_coded(out_ref, SIDE, value, True)


def rows_of(ref, at):
    return ref[rows_at(at)]


def summed(at_ref, four_ref, place, slot, mval, refs, axis, ahead, width):
    first = block_at(at_ref, axis, ahead, None) * width
    total = own_part(four_ref, place, refs[:TILES], slot, first, mval)
    refs = refs[TILES:]
    for _ in range(2):
        total = total + decoded(refs[slot][...], refs[PAIR][...], slot * SIDE + chunk_at(at_ref, axis, ahead))
        refs = refs[PAIR + 1 :]
    for state in refs:
        total = total + decoded(rows_of(state, slot), state[PAIR * ROWS :], slot)
    return total


def second_kernel(at_ref, four_ref, *rest, axis, aheads, width, terms):
    per = TILES + 2 * (PAIR + 1) + terms
    for pair, ahead in enumerate(aheads):
        refs = rest[pair * per : (pair + 1) * per]

        def value(slot, b):
            at = pair * PAIR + slot
            mval = at_ref[2 + (1 - axis) * 2 * PAIR + at]
            return summed(at_ref, four_ref, at, slot, mval, refs, axis, ahead, width)

        store_coded(rest[pair - 2], 1, value, False)


def last_kernel(at_ref, four_ref, *rest, width):
    out_ref = rest[-1]
    per = TILES + 2 * (PAIR + 1) + 2
    for group in range(GROUPS):
        refs = rest[group * per : (group + 1) * per]
        for slot in range(PAIR):
            k = group * PAIR + slot
            total = summed(at_ref, four_ref, k, slot, at_ref[2 + k], refs, 1 - group // 2, 0, width)
            out_ref[:, k, :] = total.T[:width]


def whole(array):
    return pl.BlockSpec(array.shape, lambda i, at: (0,) * array.ndim)


def four_of(slots, index):
    return pl.BlockSpec((8, slots, 2, 32, HALF), lambda i, at: (0, index, 0, 0, 0))


def second_operands(group, axis, ahead, tab, firsts, states, width):
    blocks = [functools.partial(block_at, axis=axis, ahead=ahead, b=None)]
    tab = tab[group // 2]
    specs = tile_specs(PAIR, tab.shape[1], width, group % 2, blocks)
    operands = [tab] * TILES
    for first in firsts:
        for slot in range(PAIR):
            specs.append(pl.BlockSpec((ROWS, LANES), lambda i, at, s=slot: (s * SIDE + chunk_at(at, axis, ahead), 0)))
        specs.append(pl.BlockSpec((TAIL, LANES), lambda i, at: (PAIR * SIDE * ROWS // TAIL, 0)))
        operands += [first] * (PAIR + 1)
    return specs + [whole(state) for state in states], operands + list(states)


def call(body, at, operands, in_specs, out_shapes, limit=10):
    outs = [jax.ShapeDtypeStruct(shape, dtype) for shape, dtype in out_shapes]
    return pl.pallas_call(
        body,
        grid_spec=pltpu.PrefetchScalarGridSpec(
            num_scalar_prefetch=1, grid=(1,), in_specs=in_specs, out_specs=[whole(out) for out in outs]
        ),
        out_shape=outs,
        compiler_params=pltpu.CompilerParams(vmem_limit_bytes=limit << 20),
    )(at, *operands)


def first_hop(group, ahead, at, four, tab, states, width):
    axis = group // 2
    tab = tab[axis]
    blocks = [functools.partial(block_at, axis=axis, ahead=ahead, b=b) for b in range(SIDE)]
    specs = [four_of(PAIR, group)] + tile_specs(PAIR, tab.shape[1], width, group % 2, blocks)
    specs += [whole(state) for state in states]
    operands = [four] + [tab] * (SIDE * TILES) + list(states)
    body = functools.partial(
        first_kernel, axis=axis, ahead=ahead, group=group, width=width, terms=len(states)
    )
    out = ((PAIR * SIDE * ROWS + TAIL, LANES), jnp.int16)
    return call(body, at, operands, specs, [out])[0]


def second_hop(start, aheads, at, four, tab, firsts, states, width):
    axis = 1 - start // 2
    specs, operands = [four_of(2 * PAIR, start // 2)], [four]
    for pair, ahead in enumerate(aheads):
        more, arrays = second_operands(start + pair, axis, ahead, tab, firsts[pair], states[pair], width)
        specs, operands = specs + more, operands + arrays
    body = functools.partial(second_kernel, axis=axis, aheads=aheads, width=width, terms=len(states[0]))
    return call(body, at, operands, specs, [((PAIR * ROWS + TAIL, LANES), jnp.int16)] * 2)


def last(at, four, tab, firsts, states, width):
    specs, operands = [whole(four)], [four]
    for group in range(GROUPS):
        more, arrays = second_operands(group, 1 - group // 2, 0, tab, firsts[group], states[group], width)
        specs, operands = specs + more, operands + arrays
    out = ((width, GROUPS * PAIR, ROWS), jnp.float32)
    return call(functools.partial(last_kernel, width=width), at, operands, specs, [out], 24)[0]


def ring(axis, sign):
    pairs = []
    for x in range(SIDE):
        for z in range(SIDE):
            to = ((x + sign) % SIDE, z) if axis == 0 else (x, (z + sign) % SIDE)
            pairs.append((x * SIDE + z, to[0] * SIDE + to[1]))
    return pairs


def per_device(fourier, table, wavenums):
    slots, rows, degrees = table.shape
    lat = lax.axis_size("lat")
    width = degrees // lat
    me = lax.axis_index("lat")

    split = fourier.transpose(2, 0, 3, 1)
    split = jnp.pad(split, ((0, 0), (0, 0), (0, 0), (0, HALF - rows)))
    split = split.reshape(8, slots, 2, split.shape[2], HALF)
    four = lax.all_to_all(split, "wave", split_axis=0, concat_axis=0, tiled=True)
    at = jnp.concatenate([jnp.stack([me // SIDE, me % SIDE]).astype(jnp.int32), wavenums])
    table = lax.optimization_barrier(with_layout_constraint(table, Layout((0, 1, 2))))
    table = (table[: 2 * PAIR], table[2 * PAIR :])

    def send(array, axis, sign):
        return lax.ppermute(array, "lat", ring(axis, sign))

    def first(group, ahead, states):
        return first_hop(group, ahead, at, four, table, states, width)

    def second(start, aheads, firsts, states):
        return second_hop(start, aheads, at, four, table, firsts, states, width)

    ways = [1 - 2 * (group % 2) for group in range(GROUPS)]
    every = range(GROUPS)
    far = [first(g, 2, []) for g in every]
    got_far = [send(far[g], g // 2, ways[g]) for g in every]
    near = [first(g, -ways[g], []) for g in every]
    got_near = [send(near[g], g // 2, -ways[g]) for g in every]
    both = [first(g, ways[g], [got_far[g]]) for g in every]
    got_both = [send(both[g], g // 2, ways[g]) for g in every]
    firsts = list(zip(got_near, got_both))

    halves = [(0, 1), (2, 3)]
    of = [(firsts[p], firsts[q]) for p, q in halves]
    far = [second(2 * h, (2, 2), of[h], ((), ())) for h in range(2)]
    got_far = [send(far[g // 2][g % 2], 1 - g // 2, ways[g]) for g in every]
    near = [second(2 * h, (-1, 1), of[h], ((), ())) for h in range(2)]
    got_near = [send(near[g // 2][g % 2], 1 - g // 2, -ways[g]) for g in every]
    both = [second(2 * h, (1, -1), of[h], ((got_far[p],), (got_far[q],))) for h, (p, q) in enumerate(halves)]
    got_both = [send(both[g // 2][g % 2], 1 - g // 2, ways[g]) for g in every]
    return last(at, four, table, firsts, list(zip(got_near, got_both)), width)


def solution(mesh):
    placed = (P(None, "lat", None, "wave"), P("wave", "lat", None), P("wave"))
    return jax.shard_map(
        per_device, mesh=mesh, in_specs=placed, out_specs=P("lat", "wave", None), check_vma=False
    )
```

```python
import functools

import jax
import jax.numpy as jnp
from jax import lax
from jax.experimental import pallas as pl
from jax.experimental.layout import Layout, with_layout_constraint
from jax.experimental.pallas import tpu as pltpu
from jax.sharding import PartitionSpec as P


ROWS = 256
LANES = 256
HALF = 128
TILE = 128
TILES = 3
TAIL = 16
SIDE = 4
PAIR = 2
GROUPS = 4
TOP = 32766.0
STEP = 64.0


def own_part(four_ref, slot, tiles, row, first, mval):
    tab = jnp.concatenate([tile[row] for tile in tiles], axis=1).astype(jnp.float32)
    shift = first & (TILE - 1)
    tab = pltpu.roll(tab, TILES * TILE - shift, 1)[:, :LANES]
    tab = jnp.concatenate([tab, jnp.zeros((HALF - tab.shape[0], LANES), tab.dtype)], axis=0)
    offset = lax.broadcasted_iota(jnp.int32, (1, LANES), 1) + first - mval
    keep = jnp.where(offset >= 0, 1.0, 0.0)
    sign = jnp.where((offset & 1) == 0, keep, -keep)
    tab = jnp.concatenate([(tab * keep).astype(jnp.bfloat16), (tab * sign).astype(jnp.bfloat16)], axis=0)

    def fields(hemisphere):
        held = four_ref[:, slot, hemisphere]
        held = held.reshape(ROWS, held.shape[-1])
        return jnp.concatenate([held, jnp.zeros((ROWS, HALF - held.shape[1]), held.dtype)], axis=1)

    return jnp.dot(fields(0), tab[:HALF], preferred_element_type=jnp.float32) + jnp.dot(
        fields(1), tab[HALF:], preferred_element_type=jnp.float32
    )


def decoded(codes, tail, row):
    at = lax.broadcasted_iota(jnp.int32, (TAIL, LANES), 0) == row
    code = jnp.sum(jnp.where(at, tail.astype(jnp.float32), 0.0), axis=0, keepdims=True)
    scale = jnp.exp2(code * (1.0 / STEP)) * (1.0 / TOP)
    return codes.astype(jnp.float32) * scale


def encode(value):
    most = jnp.maximum(jnp.max(jnp.abs(value), axis=0, keepdims=True), 1e-30)
    code = jnp.ceil(jnp.log2(most) * STEP) + 1.0
    inverse = jnp.exp2(code * (-1.0 / STEP)) * TOP
    return jnp.round(value * inverse).astype(jnp.int32).astype(jnp.int16), code


def rows_at(at):
    return pl.ds(at * ROWS if isinstance(at, int) else pl.multiple_of(at * ROWS, ROWS), ROWS)


def store_coded(out_ref, blocks, value, loop):
    row = lax.broadcasted_iota(jnp.int32, (TAIL, LANES), 0)

    def one(slot, tail):
        for b in range(blocks):
            at = slot * blocks + b
            codes, code = encode(value(slot, b))
            out_ref[rows_at(at)] = codes
            tail = jnp.where(row == at, code, tail)
        return tail

    tail = jnp.zeros((TAIL, LANES), jnp.float32)
    if loop:
        tail = lax.fori_loop(0, PAIR, one, tail)
    else:
        for slot in range(PAIR):
            tail = one(slot, tail)
    out_ref[PAIR * blocks * ROWS :] = tail.astype(jnp.int32).astype(jnp.int16)


def chunk_at(at, axis, ahead):
    return (at[axis] + ahead) & (SIDE - 1)


def block_at(at, axis, ahead, b):
    chunk = chunk_at(at, axis, ahead)
    other = at[1 - axis] if b is None else b
    return chunk * SIDE + other if axis == 0 else other * SIDE + chunk


def tile_specs(slots, rows, width, group, blocks):
    specs = []
    for block in blocks:
        for t in range(TILES):

            def index(i, at, block=block, t=t):
                return group, 0, block(at) * width // TILE + t

            specs.append(pl.BlockSpec((slots, rows, TILE), index))
    return specs


def first_kernel(at_ref, four_ref, *rest, axis, ahead, group, width, terms, looped):
    out_ref = rest[-1]
    tiles, states = rest[: SIDE * TILES], rest[SIDE * TILES : SIDE * TILES + terms]

    def value(slot, b):
        first = block_at(at_ref, axis, ahead, b) * width
        mval = at_ref[2 + group * PAIR + slot]
        total = own_part(four_ref, slot, tiles[b * TILES : (b + 1) * TILES], slot, first, mval)
        at = slot * SIDE + b
        for state in states:
            total = total + decoded(rows_of(state, at), state[PAIR * SIDE * ROWS :], at)
        return total

    store_coded(out_ref, SIDE, value, looped)


def rows_of(ref, at):
    return ref[rows_at(at)]


def summed(at_ref, four_ref, place, slot, mval, refs, axis, ahead, width):
    first = block_at(at_ref, axis, ahead, None) * width
    total = own_part(four_ref, place, refs[:TILES], slot, first, mval)
    refs = refs[TILES:]
    for _ in range(2):
        total = total + decoded(refs[slot][...], refs[PAIR][...], slot * SIDE + chunk_at(at_ref, axis, ahead))
        refs = refs[PAIR + 1 :]
    for state in refs:
        total = total + decoded(rows_of(state, slot), state[PAIR * ROWS :], slot)
    return total


def second_kernel(at_ref, four_ref, *rest, axis, aheads, width, terms):
    per = TILES + 2 * (PAIR + 1) + terms
    for pair, ahead in enumerate(aheads):
        refs = rest[pair * per : (pair + 1) * per]

        def value(slot, b):
            at = pair * PAIR + slot
            mval = at_ref[2 + (1 - axis) * 2 * PAIR + at]
            return summed(at_ref, four_ref, at, slot, mval, refs, axis, ahead, width)

        store_coded(rest[pair - 2], 1, value, False)


def last_kernel(at_ref, four_ref, *rest, width):
    out_ref = rest[-1]
    per = TILES + 2 * (PAIR + 1) + 2
    for group in range(GROUPS):
        refs = rest[group * per : (group + 1) * per]
        for slot in range(PAIR):
            k = group * PAIR + slot
            total = summed(at_ref, four_ref, k, slot, at_ref[2 + k], refs, 1 - group // 2, 0, width)
            out_ref[:, k, :] = total.T[:width]


def whole(array):
    return pl.BlockSpec(array.shape, lambda i, at: (0,) * array.ndim)


def four_of(four, slots, index):
    return pl.BlockSpec((8, slots, *four.shape[2:]), lambda i, at: (0, index, 0, 0, 0))


def second_operands(group, axis, ahead, tab, firsts, states, width):
    blocks = [functools.partial(block_at, axis=axis, ahead=ahead, b=None)]
    tab = tab[group // 2]
    specs = tile_specs(PAIR, tab.shape[1], width, group % 2, blocks)
    operands = [tab] * TILES
    for first in firsts:
        for slot in range(PAIR):
            specs.append(pl.BlockSpec((ROWS, LANES), lambda i, at, s=slot: (s * SIDE + chunk_at(at, axis, ahead), 0)))
        specs.append(pl.BlockSpec((TAIL, LANES), lambda i, at: (PAIR * SIDE * ROWS // TAIL, 0)))
        operands += [first] * (PAIR + 1)
    return specs + [whole(state) for state in states], operands + list(states)


def call(body, at, operands, in_specs, out_shapes, limit=10):
    outs = [jax.ShapeDtypeStruct(shape, dtype) for shape, dtype in out_shapes]
    return pl.pallas_call(
        body,
        grid_spec=pltpu.PrefetchScalarGridSpec(
            num_scalar_prefetch=1, grid=(1,), in_specs=in_specs, out_specs=[whole(out) for out in outs]
        ),
        out_shape=outs,
        compiler_params=pltpu.CompilerParams(vmem_limit_bytes=limit << 20),
    )(at, *operands)


def first_hop(group, ahead, at, four, tab, states, width):
    axis = group // 2
    tab = tab[axis]
    blocks = [functools.partial(block_at, axis=axis, ahead=ahead, b=b) for b in range(SIDE)]
    specs = [four_of(four, PAIR, group)] + tile_specs(PAIR, tab.shape[1], width, group % 2, blocks)
    specs += [whole(state) for state in states]
    operands = [four] + [tab] * (SIDE * TILES) + list(states)
    body = functools.partial(
        first_kernel, axis=axis, ahead=ahead, group=group, width=width, terms=len(states), looped=ahead != 2
    )
    out = ((PAIR * SIDE * ROWS + TAIL, LANES), jnp.int16)
    return call(body, at, operands, specs, [out])[0]


def second_hop(start, aheads, at, four, tab, firsts, states, width):
    axis = 1 - start // 2
    specs, operands = [four_of(four, 2 * PAIR, start // 2)], [four]
    for pair, ahead in enumerate(aheads):
        more, arrays = second_operands(start + pair, axis, ahead, tab, firsts[pair], states[pair], width)
        specs, operands = specs + more, operands + arrays
    body = functools.partial(second_kernel, axis=axis, aheads=aheads, width=width, terms=len(states[0]))
    return call(body, at, operands, specs, [((PAIR * ROWS + TAIL, LANES), jnp.int16)] * 2)


def last(at, four, tab, firsts, states, width):
    specs, operands = [whole(four)], [four]
    for group in range(GROUPS):
        more, arrays = second_operands(group, 1 - group // 2, 0, tab, firsts[group], states[group], width)
        specs, operands = specs + more, operands + arrays
    out = ((width, GROUPS * PAIR, ROWS), jnp.float32)
    return call(functools.partial(last_kernel, width=width), at, operands, specs, [out], 24)[0]


def ring(axis, sign):
    pairs = []
    for x in range(SIDE):
        for z in range(SIDE):
            to = ((x + sign) % SIDE, z) if axis == 0 else (x, (z + sign) % SIDE)
            pairs.append((x * SIDE + z, to[0] * SIDE + to[1]))
    return pairs


def per_device(fourier, table, wavenums):
    slots, rows, degrees = table.shape
    lat = lax.axis_size("lat")
    width = degrees // lat
    me = lax.axis_index("lat")

    split = fourier.transpose(2, 0, 3, 1)
    split = split.reshape(8, slots, 2, split.shape[2], rows)
    four = lax.all_to_all(split, "wave", split_axis=0, concat_axis=0, tiled=True)
    at = jnp.concatenate([jnp.stack([me // SIDE, me % SIDE]).astype(jnp.int32), wavenums])
    table = lax.optimization_barrier(with_layout_constraint(table, Layout((0, 1, 2))))
    table = (table[: 2 * PAIR], table[2 * PAIR :])

    def send(array, axis, sign):
        return lax.ppermute(array, "lat", ring(axis, sign))

    def first(group, ahead, states):
        return first_hop(group, ahead, at, four, table, states, width)

    def second(start, aheads, firsts, states):
        return second_hop(start, aheads, at, four, table, firsts, states, width)

    ways = [1 - 2 * (group % 2) for group in range(GROUPS)]
    every = range(GROUPS)
    far = [first(g, 2, []) for g in every]
    got_far = [send(far[g], g // 2, ways[g]) for g in every]
    near = [first(g, -ways[g], []) for g in every]
    got_near = [send(near[g], g // 2, -ways[g]) for g in every]
    both = [first(g, ways[g], [got_far[g]]) for g in every]
    got_both = [send(both[g], g // 2, ways[g]) for g in every]
    firsts = list(zip(got_near, got_both))

    halves = [(0, 1), (2, 3)]
    of = [(firsts[p], firsts[q]) for p, q in halves]
    far = [second(2 * h, (2, 2), of[h], ((), ())) for h in range(2)]
    got_far = [send(far[g // 2][g % 2], 1 - g // 2, ways[g]) for g in every]
    near = [second(2 * h, (-1, 1), of[h], ((), ())) for h in range(2)]
    got_near = [send(near[g // 2][g % 2], 1 - g // 2, -ways[g]) for g in every]
    both = [second(2 * h, (1, -1), of[h], ((got_far[p],), (got_far[q],))) for h, (p, q) in enumerate(halves)]
    got_both = [send(both[g // 2][g % 2], 1 - g // 2, ways[g]) for g in every]
    return last(at, four, table, firsts, list(zip(got_near, got_both)), width)


def solution(mesh):
    placed = (P(None, "lat", None, "wave"), P("wave", "lat", None), P("wave"))
    return jax.shard_map(
        per_device, mesh=mesh, in_specs=placed, out_specs=P("lat", "wave", None), check_vma=False
    )
```

```python
import functools

import jax
import jax.numpy as jnp
from jax import lax
from jax.experimental import pallas as pl
from jax.experimental.layout import Layout, with_layout_constraint
from jax.experimental.pallas import tpu as pltpu
from jax.sharding import PartitionSpec as P


ROWS = 256
LANES = 256
HALF = 128
TILE = 128
TILES = 3
TAIL = 16
SIDE = 4
PAIR = 2
GROUPS = 4
TOP = 32766.0
STEP = 64.0


def own_part(four_ref, slot, tiles, row, first, mval):
    tab = jnp.concatenate([tile[row] for tile in tiles], axis=1).astype(jnp.float32)
    shift = first & (TILE - 1)
    tab = pltpu.roll(tab, TILES * TILE - shift, 1)[:, :LANES]
    tab = jnp.concatenate([tab, jnp.zeros((HALF - tab.shape[0], LANES), tab.dtype)], axis=0)
    offset = lax.broadcasted_iota(jnp.int32, (1, LANES), 1) + first - mval
    keep = jnp.where(offset >= 0, 1.0, 0.0)
    sign = jnp.where((offset & 1) == 0, keep, -keep)
    tab = jnp.concatenate([(tab * keep).astype(jnp.bfloat16), (tab * sign).astype(jnp.bfloat16)], axis=0)

    def fields(hemisphere):
        held = four_ref[:, slot, hemisphere]
        held = held.reshape(ROWS, held.shape[-1])
        return jnp.concatenate([held, jnp.zeros((ROWS, HALF - held.shape[1]), held.dtype)], axis=1)

    return jnp.dot(fields(0), tab[:HALF], preferred_element_type=jnp.float32) + jnp.dot(
        fields(1), tab[HALF:], preferred_element_type=jnp.float32
    )


def decoded(codes, tail, row):
    at = lax.broadcasted_iota(jnp.int32, (TAIL, LANES), 0) == row
    code = jnp.sum(jnp.where(at, tail.astype(jnp.float32), 0.0), axis=0, keepdims=True)
    scale = jnp.exp2(code * (1.0 / STEP)) * (1.0 / TOP)
    return codes.astype(jnp.float32) * scale


def encode(value):
    most = jnp.maximum(jnp.max(jnp.abs(value), axis=0, keepdims=True), 1e-30)
    code = jnp.ceil(jnp.log2(most) * STEP) + 1.0
    inverse = jnp.exp2(code * (-1.0 / STEP)) * TOP
    return jnp.round(value * inverse).astype(jnp.int32).astype(jnp.int16), code


def rows_at(at):
    return pl.ds(at * ROWS if isinstance(at, int) else pl.multiple_of(at * ROWS, ROWS), ROWS)


def store_coded(out_ref, blocks, value, loop):
    row = lax.broadcasted_iota(jnp.int32, (TAIL, LANES), 0)

    def one(slot, tail):
        for b in range(blocks):
            at = slot * blocks + b
            codes, code = encode(value(slot, b))
            out_ref[rows_at(at)] = codes
            tail = jnp.where(row == at, code, tail)
        return tail

    tail = jnp.zeros((TAIL, LANES), jnp.float32)
    if loop:
        tail = lax.fori_loop(0, PAIR, one, tail)
    else:
        for slot in range(PAIR):
            tail = one(slot, tail)
    out_ref[PAIR * blocks * ROWS :] = tail.astype(jnp.int32).astype(jnp.int16)


def chunk_at(at, axis, ahead):
    return (at[axis] + ahead) & (SIDE - 1)


def block_at(at, axis, ahead, b):
    chunk = chunk_at(at, axis, ahead)
    other = at[1 - axis] if b is None else b
    return chunk * SIDE + other if axis == 0 else other * SIDE + chunk


def tile_specs(slots, rows, width, group, blocks):
    specs = []
    for block in blocks:
        for t in range(TILES):

            def index(i, at, block=block, t=t):
                return group, 0, block(at) * width // TILE + t

            specs.append(pl.BlockSpec((slots, rows, TILE), index))
    return specs


def first_kernel(at_ref, four_ref, *rest, axis, ahead, group, width, terms, looped):
    out_ref = rest[-1]
    tiles, states = rest[: SIDE * TILES], rest[SIDE * TILES : SIDE * TILES + terms]

    def value(slot, b):
        first = block_at(at_ref, axis, ahead, b) * width
        mval = at_ref[2 + group * PAIR + slot]
        total = own_part(four_ref, slot, tiles[b * TILES : (b + 1) * TILES], slot, first, mval)
        at = slot * SIDE + b
        for state in states:
            total = total + decoded(rows_of(state, at), state[PAIR * SIDE * ROWS :], at)
        return total

    store_coded(out_ref, SIDE, value, looped)


def rows_of(ref, at):
    return ref[rows_at(at)]


def summed(at_ref, four_ref, place, slot, mval, refs, axis, ahead, width):
    first = block_at(at_ref, axis, ahead, None) * width
    total = own_part(four_ref, place, refs[:TILES], slot, first, mval)
    refs = refs[TILES:]
    for _ in range(2):
        total = total + decoded(refs[slot][...], refs[PAIR][...], slot * SIDE + chunk_at(at_ref, axis, ahead))
        refs = refs[PAIR + 1 :]
    for state in refs:
        total = total + decoded(rows_of(state, slot), state[PAIR * ROWS :], slot)
    return total


def second_kernel(at_ref, four_ref, *rest, axis, aheads, width, terms):
    per = TILES + 2 * (PAIR + 1) + terms
    for pair, ahead in enumerate(aheads):
        refs = rest[pair * per : (pair + 1) * per]

        def value(slot, b):
            at = pair * PAIR + slot
            mval = at_ref[2 + (1 - axis) * 2 * PAIR + at]
            return summed(at_ref, four_ref, at, slot, mval, refs, axis, ahead, width)

        store_coded(rest[pair - 2], 1, value, False)


def last_kernel(at_ref, four_ref, *rest, start, width):
    out_ref = rest[-1]
    per = TILES + 2 * (PAIR + 1) + 2
    if start:
        out_ref[:, : start * PAIR] = rest[2 * per][...]
    for pair in range(2):
        refs = rest[pair * per : (pair + 1) * per]
        for slot in range(PAIR):
            at = pair * PAIR + slot
            k = start * PAIR + at
            total = summed(at_ref, four_ref, at, slot, at_ref[2 + k], refs, 1 - start // 2, 0, width)
            out_ref[:, k, :] = total.T[:width]


def whole(array):
    return pl.BlockSpec(array.shape, lambda i, at: (0,) * array.ndim)


def four_of(four, slots, index):
    return pl.BlockSpec((8, slots, *four.shape[2:]), lambda i, at: (0, index, 0, 0, 0))


def second_operands(group, axis, ahead, tab, firsts, states, width):
    blocks = [functools.partial(block_at, axis=axis, ahead=ahead, b=None)]
    tab = tab[group // 2]
    specs = tile_specs(PAIR, tab.shape[1], width, group % 2, blocks)
    operands = [tab] * TILES
    for first in firsts:
        for slot in range(PAIR):
            specs.append(pl.BlockSpec((ROWS, LANES), lambda i, at, s=slot: (s * SIDE + chunk_at(at, axis, ahead), 0)))
        specs.append(pl.BlockSpec((TAIL, LANES), lambda i, at: (PAIR * SIDE * ROWS // TAIL, 0)))
        operands += [first] * (PAIR + 1)
    return specs + [whole(state) for state in states], operands + list(states)


def call(body, at, operands, in_specs, out_shapes, limit=10):
    outs = [jax.ShapeDtypeStruct(shape, dtype) for shape, dtype in out_shapes]
    return pl.pallas_call(
        body,
        grid_spec=pltpu.PrefetchScalarGridSpec(
            num_scalar_prefetch=1, grid=(1,), in_specs=in_specs, out_specs=[whole(out) for out in outs]
        ),
        out_shape=outs,
        compiler_params=pltpu.CompilerParams(vmem_limit_bytes=limit << 20),
    )(at, *operands)


def first_hop(group, ahead, at, four, tab, states, width):
    axis = group // 2
    tab = tab[axis]
    blocks = [functools.partial(block_at, axis=axis, ahead=ahead, b=b) for b in range(SIDE)]
    specs = [four_of(four, PAIR, group)] + tile_specs(PAIR, tab.shape[1], width, group % 2, blocks)
    specs += [whole(state) for state in states]
    operands = [four] + [tab] * (SIDE * TILES) + list(states)
    body = functools.partial(
        first_kernel, axis=axis, ahead=ahead, group=group, width=width, terms=len(states), looped=ahead != 2
    )
    out = ((PAIR * SIDE * ROWS + TAIL, LANES), jnp.int16)
    return call(body, at, operands, specs, [out])[0]


def second_hop(start, aheads, at, four, tab, firsts, states, width):
    axis = 1 - start // 2
    specs, operands = [four_of(four, 2 * PAIR, start // 2)], [four]
    for pair, ahead in enumerate(aheads):
        more, arrays = second_operands(start + pair, axis, ahead, tab, firsts[pair], states[pair], width)
        specs, operands = specs + more, operands + arrays
    body = functools.partial(second_kernel, axis=axis, aheads=aheads, width=width, terms=len(states[0]))
    return call(body, at, operands, specs, [((PAIR * ROWS + TAIL, LANES), jnp.int16)] * 2)


def last(start, at, four, tab, firsts, states, others, width):
    specs, operands = [four_of(four, 2 * PAIR, start // 2)], [four]
    for group in (start, start + 1):
        more, arrays = second_operands(group, 1 - start // 2, 0, tab, firsts[group], states[group], width)
        specs, operands = specs + more, operands + arrays
    specs, operands = specs + [whole(other) for other in others], operands + others
    out = ((width, (start + 2) * PAIR, ROWS), jnp.float32)
    body = functools.partial(last_kernel, start=start, width=width)
    return call(body, at, operands, specs, [out], 20)[0]


def ring(axis, sign):
    pairs = []
    for x in range(SIDE):
        for z in range(SIDE):
            to = ((x + sign) % SIDE, z) if axis == 0 else (x, (z + sign) % SIDE)
            pairs.append((x * SIDE + z, to[0] * SIDE + to[1]))
    return pairs


def per_device(fourier, table, wavenums):
    slots, rows, degrees = table.shape
    lat = lax.axis_size("lat")
    width = degrees // lat
    me = lax.axis_index("lat")

    split = fourier.transpose(2, 0, 3, 1)
    split = split.reshape(8, slots, 2, split.shape[2], rows)
    four = lax.all_to_all(split, "wave", split_axis=0, concat_axis=0, tiled=True)
    at = jnp.concatenate([jnp.stack([me // SIDE, me % SIDE]).astype(jnp.int32), wavenums])
    table = lax.optimization_barrier(with_layout_constraint(table, Layout((0, 1, 2))))
    half = table[: 2 * PAIR]
    table, half = lax.optimization_barrier((table, half))
    table = (half, table[2 * PAIR :])

    def send(array, axis, sign):
        return lax.ppermute(array, "lat", ring(axis, sign))

    def first(group, ahead, states):
        return first_hop(group, ahead, at, four, table, states, width)

    def second(start, aheads, firsts, states):
        return second_hop(start, aheads, at, four, table, firsts, states, width)

    ways = [1 - 2 * (group % 2) for group in range(GROUPS)]
    every = range(GROUPS)
    far = [first(g, 2, []) for g in every]
    got_far = [send(far[g], g // 2, ways[g]) for g in every]
    near = [first(g, -ways[g], []) for g in every]
    got_near = [send(near[g], g // 2, -ways[g]) for g in every]
    both = [first(g, ways[g], [got_far[g]]) for g in every]
    got_both = [send(both[g], g // 2, ways[g]) for g in every]
    firsts = list(zip(got_near, got_both))

    halves = [(0, 1), (2, 3)]
    of = [(firsts[p], firsts[q]) for p, q in halves]
    far = [second(2 * h, (2, 2), of[h], ((), ())) for h in range(2)]
    got_far = [send(far[g // 2][g % 2], 1 - g // 2, ways[g]) for g in every]
    near = [second(2 * h, (-1, 1), of[h], ((), ())) for h in range(2)]
    got_near = [send(near[g // 2][g % 2], 1 - g // 2, -ways[g]) for g in every]
    both = [second(2 * h, (1, -1), of[h], ((got_far[p],), (got_far[q],))) for h, (p, q) in enumerate(halves)]
    got_both = [send(both[g // 2][g % 2], 1 - g // 2, ways[g]) for g in every]
    states = list(zip(got_near, got_both))
    part = last(0, at, four, table, firsts, states, [], width)
    return last(2, at, four, table, firsts, states, [part], width)


def solution(mesh):
    placed = (P(None, "lat", None, "wave"), P("wave", "lat", None), P("wave"))
    return jax.shard_map(
        per_device, mesh=mesh, in_specs=placed, out_specs=P("lat", "wave", None), check_vma=False
    )
```

```python
import functools

import jax
import jax.numpy as jnp
from jax import lax
from jax.experimental import pallas as pl
from jax.experimental.layout import Layout, with_layout_constraint
from jax.experimental.pallas import tpu as pltpu
from jax.sharding import PartitionSpec as P


ROWS = 256
LANES = 256
HALF = 128
TILE = 128
TILES = 3
TAIL = 16
SIDE = 4
PAIR = 2
GROUPS = 4
TOP = 32766.0
STEP = 64.0


def own_part(four_ref, slot, tiles, row, first, mval):
    tab = jnp.concatenate([tile[row] for tile in tiles], axis=1).astype(jnp.float32)
    shift = first & (TILE - 1)
    tab = pltpu.roll(tab, TILES * TILE - shift, 1)[:, :LANES]
    tab = jnp.concatenate([tab, jnp.zeros((HALF - tab.shape[0], LANES), tab.dtype)], axis=0)
    offset = lax.broadcasted_iota(jnp.int32, (1, LANES), 1) + first - mval
    keep = jnp.where(offset >= 0, 1.0, 0.0)
    sign = jnp.where((offset & 1) == 0, keep, -keep)
    tab = jnp.concatenate([(tab * keep).astype(jnp.bfloat16), (tab * sign).astype(jnp.bfloat16)], axis=0)

    def fields(hemisphere):
        held = four_ref[:, slot, hemisphere]
        held = held.reshape(ROWS, held.shape[-1])
        return jnp.concatenate([held, jnp.zeros((ROWS, HALF - held.shape[1]), held.dtype)], axis=1)

    return jnp.dot(fields(0), tab[:HALF], preferred_element_type=jnp.float32) + jnp.dot(
        fields(1), tab[HALF:], preferred_element_type=jnp.float32
    )


def decoded(codes, tail, row):
    at = lax.broadcasted_iota(jnp.int32, (TAIL, LANES), 0) == row
    code = jnp.sum(jnp.where(at, tail.astype(jnp.float32), 0.0), axis=0, keepdims=True)
    scale = jnp.exp2(code * (1.0 / STEP)) * (1.0 / TOP)
    return codes.astype(jnp.float32) * scale


def encode(value):
    most = jnp.maximum(jnp.max(jnp.abs(value), axis=0, keepdims=True), 1e-30)
    code = jnp.ceil(jnp.log2(most) * STEP) + 1.0
    inverse = jnp.exp2(code * (-1.0 / STEP)) * TOP
    return jnp.round(value * inverse).astype(jnp.int32).astype(jnp.int16), code


def rows_at(at):
    return pl.ds(at * ROWS if isinstance(at, int) else pl.multiple_of(at * ROWS, ROWS), ROWS)


def store_coded(out_ref, blocks, value, loop):
    row = lax.broadcasted_iota(jnp.int32, (TAIL, LANES), 0)

    def one(slot, tail):
        for b in range(blocks):
            at = slot * blocks + b
            codes, code = encode(value(slot, b))
            out_ref[rows_at(at)] = codes
            tail = jnp.where(row == at, code, tail)
        return tail

    tail = jnp.zeros((TAIL, LANES), jnp.float32)
    if loop:
        tail = lax.fori_loop(0, PAIR, one, tail)
    else:
        for slot in range(PAIR):
            tail = one(slot, tail)
    out_ref[PAIR * blocks * ROWS :] = tail.astype(jnp.int32).astype(jnp.int16)


def chunk_at(at, axis, ahead):
    return (at[axis] + ahead) & (SIDE - 1)


def block_at(at, axis, ahead, b):
    chunk = chunk_at(at, axis, ahead)
    other = at[1 - axis] if b is None else b
    return chunk * SIDE + other if axis == 0 else other * SIDE + chunk


def tile_specs(slots, rows, width, group, blocks):
    specs = []
    for block in blocks:
        for t in range(TILES):

            def index(i, at, block=block, t=t):
                return group, 0, block(at) * width // TILE + t

            specs.append(pl.BlockSpec((slots, rows, TILE), index))
    return specs


def first_kernel(at_ref, four_ref, *rest, axis, ahead, group, width, terms, looped):
    out_ref = rest[-1]
    tiles, states = rest[: SIDE * TILES], rest[SIDE * TILES : SIDE * TILES + terms]

    def value(slot, b):
        first = block_at(at_ref, axis, ahead, b) * width
        mval = at_ref[2 + group * PAIR + slot]
        total = own_part(four_ref, slot, tiles[b * TILES : (b + 1) * TILES], slot, first, mval)
        at = slot * SIDE + b
        for state in states:
            total = total + decoded(rows_of(state, at), state[PAIR * SIDE * ROWS :], at)
        return total

    store_coded(out_ref, SIDE, value, looped)


def rows_of(ref, at):
    return ref[rows_at(at)]


def summed(at_ref, four_ref, place, slot, mval, refs, axis, ahead, width):
    first = block_at(at_ref, axis, ahead, None) * width
    total = own_part(four_ref, place, refs[:TILES], slot, first, mval)
    refs = refs[TILES:]
    for _ in range(2):
        total = total + decoded(refs[slot][...], refs[PAIR][...], slot * SIDE + chunk_at(at_ref, axis, ahead))
        refs = refs[PAIR + 1 :]
    for state in refs:
        total = total + decoded(rows_of(state, slot), state[PAIR * ROWS :], slot)
    return total


def second_kernel(at_ref, four_ref, *rest, axis, jobs, width, terms):
    per = TILES + 2 * (PAIR + 1) + terms
    for job, (pair, ahead) in enumerate(jobs):
        refs = rest[job * per : (job + 1) * per]

        def value(slot, b):
            at = pair * PAIR + slot
            mval = at_ref[2 + (1 - axis) * 2 * PAIR + at]
            return summed(at_ref, four_ref, at, slot, mval, refs, axis, ahead, width)

        store_coded(rest[job - len(jobs)], 1, value, False)


def last_kernel(at_ref, four_ref, *rest, start, width):
    out_ref = rest[-1]
    per = TILES + 2 * (PAIR + 1) + 2
    if start:
        out_ref[:, : start * PAIR] = rest[2 * per][...]
    for pair in range(2):
        refs = rest[pair * per : (pair + 1) * per]
        for slot in range(PAIR):
            at = pair * PAIR + slot
            k = start * PAIR + at
            total = summed(at_ref, four_ref, at, slot, at_ref[2 + k], refs, 1 - start // 2, 0, width)
            out_ref[:, k, :] = total.T[:width]


def whole(array):
    return pl.BlockSpec(array.shape, lambda i, at: (0,) * array.ndim)


def four_of(four, slots, index):
    return pl.BlockSpec((8, slots, *four.shape[2:]), lambda i, at: (0, index, 0, 0, 0))


def second_operands(group, axis, ahead, tab, firsts, states, width):
    blocks = [functools.partial(block_at, axis=axis, ahead=ahead, b=None)]
    tab = tab[group // 2]
    specs = tile_specs(PAIR, tab.shape[1], width, group % 2, blocks)
    operands = [tab] * TILES
    for first in firsts:
        for slot in range(PAIR):
            specs.append(pl.BlockSpec((ROWS, LANES), lambda i, at, s=slot: (s * SIDE + chunk_at(at, axis, ahead), 0)))
        specs.append(pl.BlockSpec((TAIL, LANES), lambda i, at: (PAIR * SIDE * ROWS // TAIL, 0)))
        operands += [first] * (PAIR + 1)
    return specs + [whole(state) for state in states], operands + list(states)


def call(body, at, operands, in_specs, out_shapes, limit=10):
    outs = [jax.ShapeDtypeStruct(shape, dtype) for shape, dtype in out_shapes]
    return pl.pallas_call(
        body,
        grid_spec=pltpu.PrefetchScalarGridSpec(
            num_scalar_prefetch=1, grid=(1,), in_specs=in_specs, out_specs=[whole(out) for out in outs]
        ),
        out_shape=outs,
        compiler_params=pltpu.CompilerParams(vmem_limit_bytes=limit << 20),
    )(at, *operands)


def first_hop(group, ahead, at, four, tab, states, width):
    axis = group // 2
    tab = tab[axis]
    blocks = [functools.partial(block_at, axis=axis, ahead=ahead, b=b) for b in range(SIDE)]
    specs = [four_of(four, PAIR, group)] + tile_specs(PAIR, tab.shape[1], width, group % 2, blocks)
    specs += [whole(state) for state in states]
    operands = [four] + [tab] * (SIDE * TILES) + list(states)
    body = functools.partial(
        first_kernel, axis=axis, ahead=ahead, group=group, width=width, terms=len(states), looped=ahead != 2
    )
    out = ((PAIR * SIDE * ROWS + TAIL, LANES), jnp.int16)
    return call(body, at, operands, specs, [out])[0]


def second_hop(start, jobs, at, four, tab, firsts, states, width):
    axis = 1 - start // 2
    specs, operands = [four_of(four, 2 * PAIR, start // 2)], [four]
    for (pair, ahead), sums in zip(jobs, states):
        more, arrays = second_operands(start + pair, axis, ahead, tab, firsts[pair], sums, width)
        specs, operands = specs + more, operands + arrays
    body = functools.partial(second_kernel, axis=axis, jobs=jobs, width=width, terms=len(states[0]))
    return call(body, at, operands, specs, [((PAIR * ROWS + TAIL, LANES), jnp.int16)] * len(jobs))


def last(start, at, four, tab, firsts, states, others, width):
    specs, operands = [four_of(four, 2 * PAIR, start // 2)], [four]
    for group in (start, start + 1):
        more, arrays = second_operands(group, 1 - start // 2, 0, tab, firsts[group], states[group], width)
        specs, operands = specs + more, operands + arrays
    specs, operands = specs + [whole(other) for other in others], operands + others
    out = ((width, (start + 2) * PAIR, ROWS), jnp.float32)
    body = functools.partial(last_kernel, start=start, width=width)
    return call(body, at, operands, specs, [out], 20)[0]


def ring(axis, sign):
    pairs = []
    for x in range(SIDE):
        for z in range(SIDE):
            to = ((x + sign) % SIDE, z) if axis == 0 else (x, (z + sign) % SIDE)
            pairs.append((x * SIDE + z, to[0] * SIDE + to[1]))
    return pairs


def per_device(fourier, table, wavenums):
    slots, rows, degrees = table.shape
    lat = lax.axis_size("lat")
    width = degrees // lat
    me = lax.axis_index("lat")

    split = fourier.transpose(2, 0, 3, 1)
    split = split.reshape(8, slots, 2, split.shape[2], rows)
    four = lax.all_to_all(split, "wave", split_axis=0, concat_axis=0, tiled=True)
    at = jnp.concatenate([jnp.stack([me // SIDE, me % SIDE]).astype(jnp.int32), wavenums])
    table = lax.optimization_barrier(with_layout_constraint(table, Layout((0, 1, 2))))
    half = table[: 2 * PAIR]
    table, half = lax.optimization_barrier((table, half))
    table = (half, table[2 * PAIR :])

    def send(array, axis, sign):
        return lax.ppermute(array, "lat", ring(axis, sign))

    def first(group, ahead, states):
        return first_hop(group, ahead, at, four, table, states, width)

    def second(start, jobs, firsts, states):
        return second_hop(start, jobs, at, four, table, firsts, states, width)

    ways = [1 - 2 * (group % 2) for group in range(GROUPS)]
    every = range(GROUPS)
    far = [first(g, 2, []) for g in every]
    got_far = [send(far[g], g // 2, ways[g]) for g in every]
    near = [first(g, -ways[g], []) for g in every]
    got_near = [send(near[g], g // 2, -ways[g]) for g in every]
    both = [first(g, ways[g], [got_far[g]]) for g in every]
    got_both = [send(both[g], g // 2, ways[g]) for g in every]
    firsts = list(zip(got_near, got_both))

    halves = [(0, 1), (2, 3)]
    of = [(firsts[p], firsts[q]) for p, q in halves]
    jobs = ((0, 2), (1, 2), (0, -1), (1, 1))
    alone = [second(2 * h, jobs, of[h], ((),) * 4) for h in range(2)]
    got_far = [send(alone[g // 2][g % 2], 1 - g // 2, ways[g]) for g in every]
    got_near = [send(alone[g // 2][2 + g % 2], 1 - g // 2, -ways[g]) for g in every]
    both = [second(2 * h, ((0, 1), (1, -1)), of[h], ((got_far[p],), (got_far[q],))) for h, (p, q) in enumerate(halves)]
    got_both = [send(both[g // 2][g % 2], 1 - g // 2, ways[g]) for g in every]
    states = list(zip(got_near, got_both))
    part = last(0, at, four, table, firsts, states, [], width)
    return last(2, at, four, table, firsts, states, [part], width)


def solution(mesh):
    placed = (P(None, "lat", None, "wave"), P("wave", "lat", None), P("wave"))
    return jax.shard_map(
        per_device, mesh=mesh, in_specs=placed, out_specs=P("lat", "wave", None), check_vma=False
    )
```

```python
import functools

import jax
import jax.numpy as jnp
from jax import lax
from jax.experimental import pallas as pl
from jax.experimental.layout import Layout, with_layout_constraint
from jax.experimental.pallas import tpu as pltpu
from jax.sharding import PartitionSpec as P


ROWS = 256
LANES = 256
HALF = 128
TILE = 128
TILES = 3
TAIL = 16
SIDE = 4
WAVENUMS = 4
PAIR = 2
GROUPS = 4
TOP = 32766.0
STEP = 64.0


def own_part(four_ref, slot, tiles, row, first, mval):
    tab = jnp.concatenate([tile[row] for tile in tiles], axis=1).astype(jnp.float32)
    shift = first & (TILE - 1)
    tab = pltpu.roll(tab, TILES * TILE - shift, 1)[:, :LANES]
    tab = jnp.concatenate([tab, jnp.zeros((HALF - tab.shape[0], LANES), tab.dtype)], axis=0)
    offset = lax.broadcasted_iota(jnp.int32, (1, LANES), 1) + first - mval
    keep = jnp.where(offset >= 0, 1.0, 0.0)
    sign = jnp.where((offset & 1) == 0, keep, -keep)
    tab = jnp.concatenate([(tab * keep).astype(jnp.bfloat16), (tab * sign).astype(jnp.bfloat16)], axis=0)

    def fields(hemisphere):
        held = four_ref[:, slot, hemisphere]
        held = held.reshape(ROWS, held.shape[-1])
        return jnp.concatenate([held, jnp.zeros((ROWS, HALF - held.shape[1]), held.dtype)], axis=1)

    return jnp.dot(fields(0), tab[:HALF], preferred_element_type=jnp.float32) + jnp.dot(
        fields(1), tab[HALF:], preferred_element_type=jnp.float32
    )


def decoded(codes, tail, row):
    at = lax.broadcasted_iota(jnp.int32, (TAIL, LANES), 0) == row
    code = jnp.sum(jnp.where(at, tail.astype(jnp.float32), 0.0), axis=0, keepdims=True)
    scale = jnp.exp2(code * (1.0 / STEP)) * (1.0 / TOP)
    return codes.astype(jnp.float32) * scale


def encode(value):
    most = jnp.maximum(jnp.max(jnp.abs(value), axis=0, keepdims=True), 1e-30)
    code = jnp.ceil(jnp.log2(most) * STEP) + 1.0
    inverse = jnp.exp2(code * (-1.0 / STEP)) * TOP
    return jnp.round(value * inverse).astype(jnp.int32).astype(jnp.int16), code


def rows_at(at):
    return pl.ds(at * ROWS if isinstance(at, int) else pl.multiple_of(at * ROWS, ROWS), ROWS)


def store_coded(out_ref, blocks, value, loop):
    row = lax.broadcasted_iota(jnp.int32, (TAIL, LANES), 0)

    def one(slot, tail):
        for b in range(blocks):
            at = slot * blocks + b
            codes, code = encode(value(slot, b))
            out_ref[rows_at(at)] = codes
            tail = jnp.where(row == at, code, tail)
        return tail

    tail = jnp.zeros((TAIL, LANES), jnp.float32)
    if loop:
        tail = lax.fori_loop(0, PAIR, one, tail)
    else:
        for slot in range(PAIR):
            tail = one(slot, tail)
    out_ref[PAIR * blocks * ROWS :] = tail.astype(jnp.int32).astype(jnp.int16)


def chunk_at(at, axis, ahead):
    return (at[axis] + ahead) & (SIDE - 1)


def block_at(at, axis, ahead, b):
    chunk = chunk_at(at, axis, ahead)
    other = at[1 - axis] if b is None else b
    return chunk * at[2 + axis] + other * at[3 - axis]


def tile_specs(slots, rows, width, group, blocks):
    specs = []
    for block in blocks:
        for t in range(TILES):

            def index(i, at, block=block, t=t):
                return group, 0, block(at) * width // TILE + t

            specs.append(pl.BlockSpec((slots, rows, TILE), index))
    return specs


def first_kernel(at_ref, four_ref, *rest, axis, ahead, group, width, terms, looped):
    out_ref = rest[-1]
    tiles, states = rest[: SIDE * TILES], rest[SIDE * TILES : SIDE * TILES + terms]

    def value(slot, b):
        first = block_at(at_ref, axis, ahead, b) * width
        mval = at_ref[WAVENUMS + group * PAIR + slot]
        total = own_part(four_ref, slot, tiles[b * TILES : (b + 1) * TILES], slot, first, mval)
        at = slot * SIDE + b
        for state in states:
            total = total + decoded(rows_of(state, at), state[PAIR * SIDE * ROWS :], at)
        return total

    store_coded(out_ref, SIDE, value, looped)


def rows_of(ref, at):
    return ref[rows_at(at)]


def summed(at_ref, four_ref, place, slot, mval, refs, axis, ahead, width):
    first = block_at(at_ref, axis, ahead, None) * width
    total = own_part(four_ref, place, refs[:TILES], slot, first, mval)
    refs = refs[TILES:]
    for _ in range(2):
        total = total + decoded(refs[slot][...], refs[PAIR][...], slot * SIDE + chunk_at(at_ref, axis, ahead))
        refs = refs[PAIR + 1 :]
    for state in refs:
        total = total + decoded(rows_of(state, slot), state[PAIR * ROWS :], slot)
    return total


def second_kernel(at_ref, four_ref, *rest, axis, jobs, width, terms):
    per = TILES + 2 * (PAIR + 1) + terms
    for job, (pair, ahead) in enumerate(jobs):
        refs = rest[job * per : (job + 1) * per]

        def value(slot, b):
            at = pair * PAIR + slot
            mval = at_ref[WAVENUMS + (1 - axis) * 2 * PAIR + at]
            return summed(at_ref, four_ref, at, slot, mval, refs, axis, ahead, width)

        store_coded(rest[job - len(jobs)], 1, value, False)


def last_kernel(at_ref, four_ref, *rest, start, width):
    out_ref = rest[-1]
    per = TILES + 2 * (PAIR + 1) + 2
    if start:
        out_ref[:, : start * PAIR] = rest[2 * per][...]
    for pair in range(2):
        refs = rest[pair * per : (pair + 1) * per]
        for slot in range(PAIR):
            at = pair * PAIR + slot
            k = start * PAIR + at
            total = summed(at_ref, four_ref, at, slot, at_ref[WAVENUMS + k], refs, 1 - start // 2, 0, width)
            out_ref[:, k, :] = total.T[:width]


def whole(array):
    return pl.BlockSpec(array.shape, lambda i, at: (0,) * array.ndim)


def four_of(four, slots, index):
    return pl.BlockSpec((8, slots, *four.shape[2:]), lambda i, at: (0, index, 0, 0, 0))


def second_operands(group, axis, ahead, tab, firsts, states, width):
    blocks = [functools.partial(block_at, axis=axis, ahead=ahead, b=None)]
    tab = tab[group // 2]
    specs = tile_specs(PAIR, tab.shape[1], width, group % 2, blocks)
    operands = [tab] * TILES
    for first in firsts:
        for slot in range(PAIR):
            specs.append(pl.BlockSpec((ROWS, LANES), lambda i, at, s=slot: (s * SIDE + chunk_at(at, axis, ahead), 0)))
        specs.append(pl.BlockSpec((TAIL, LANES), lambda i, at: (PAIR * SIDE * ROWS // TAIL, 0)))
        operands += [first] * (PAIR + 1)
    return specs + [whole(state) for state in states], operands + list(states)


def call(body, at, operands, in_specs, out_shapes, limit=10):
    outs = [jax.ShapeDtypeStruct(shape, dtype) for shape, dtype in out_shapes]
    return pl.pallas_call(
        body,
        grid_spec=pltpu.PrefetchScalarGridSpec(
            num_scalar_prefetch=1, grid=(1,), in_specs=in_specs, out_specs=[whole(out) for out in outs]
        ),
        out_shape=outs,
        compiler_params=pltpu.CompilerParams(vmem_limit_bytes=limit << 20),
    )(at, *operands)


def first_hop(group, ahead, at, four, tab, states, width):
    axis = group // 2
    tab = tab[axis]
    blocks = [functools.partial(block_at, axis=axis, ahead=ahead, b=b) for b in range(SIDE)]
    specs = [four_of(four, PAIR, group)] + tile_specs(PAIR, tab.shape[1], width, group % 2, blocks)
    specs += [whole(state) for state in states]
    operands = [four] + [tab] * (SIDE * TILES) + list(states)
    body = functools.partial(
        first_kernel, axis=axis, ahead=ahead, group=group, width=width, terms=len(states), looped=ahead != 2
    )
    out = ((PAIR * SIDE * ROWS + TAIL, LANES), jnp.int16)
    return call(body, at, operands, specs, [out])[0]


def second_hop(start, jobs, at, four, tab, firsts, states, width):
    axis = 1 - start // 2
    specs, operands = [four_of(four, 2 * PAIR, start // 2)], [four]
    for (pair, ahead), sums in zip(jobs, states):
        more, arrays = second_operands(start + pair, axis, ahead, tab, firsts[pair], sums, width)
        specs, operands = specs + more, operands + arrays
    body = functools.partial(second_kernel, axis=axis, jobs=jobs, width=width, terms=len(states[0]))
    return call(body, at, operands, specs, [((PAIR * ROWS + TAIL, LANES), jnp.int16)] * len(jobs))


def last(start, at, four, tab, firsts, states, others, width):
    specs, operands = [four_of(four, 2 * PAIR, start // 2)], [four]
    for group in (start, start + 1):
        more, arrays = second_operands(group, 1 - start // 2, 0, tab, firsts[group], states[group], width)
        specs, operands = specs + more, operands + arrays
    specs, operands = specs + [whole(other) for other in others], operands + others
    out = ((width, (start + 2) * PAIR, ROWS), jnp.float32)
    body = functools.partial(last_kernel, start=start, width=width)
    return call(body, at, operands, specs, [out], 20)[0]


def ring(axis, sign):
    pairs = []
    for x in range(SIDE):
        for z in range(SIDE):
            for wave in range(8):
                to = ((x + sign) % SIDE, z) if axis == wave % 2 else (x, (z + sign) % SIDE)
                pairs.append(((x * SIDE + z) * 8 + wave, (to[0] * SIDE + to[1]) * 8 + wave))
    return pairs


def per_device(fourier, table, wavenums):
    slots, rows, degrees = table.shape
    lat = lax.axis_size("lat")
    width = degrees // lat
    me = lax.axis_index("lat")

    split = fourier.transpose(2, 0, 3, 1)
    split = split.reshape(8, slots, 2, split.shape[2], rows)
    four = lax.all_to_all(split, "wave", split_axis=0, concat_axis=0, tiled=True)
    swapped = lax.axis_index("wave") % 2 == 1
    x, z = me // SIDE, me % SIDE
    places = [jnp.where(swapped, z, x), jnp.where(swapped, x, z)]
    strides = [jnp.where(swapped, 1, SIDE), jnp.where(swapped, SIDE, 1)]
    at = jnp.concatenate([jnp.stack(places + strides).astype(jnp.int32), wavenums])
    table = lax.optimization_barrier(with_layout_constraint(table, Layout((0, 1, 2))))
    half = table[: 2 * PAIR]
    table, half = lax.optimization_barrier((table, half))
    table = (half, table[2 * PAIR :])

    def send(array, axis, sign):
        return lax.ppermute(array, ("lat", "wave"), ring(axis, sign))

    def first(group, ahead, states):
        return first_hop(group, ahead, at, four, table, states, width)

    def second(start, jobs, firsts, states):
        return second_hop(start, jobs, at, four, table, firsts, states, width)

    ways = [1 - 2 * (group % 2) for group in range(GROUPS)]
    every = range(GROUPS)
    far = [first(g, 2, []) for g in every]
    got_far = [send(far[g], g // 2, ways[g]) for g in every]
    near = [first(g, -ways[g], []) for g in every]
    got_near = [send(near[g], g // 2, -ways[g]) for g in every]
    both = [first(g, ways[g], [got_far[g]]) for g in every]
    got_both = [send(both[g], g // 2, ways[g]) for g in every]
    firsts = list(zip(got_near, got_both))

    halves = [(0, 1), (2, 3)]
    of = [(firsts[p], firsts[q]) for p, q in halves]
    jobs = ((0, 2), (1, 2), (0, -1), (1, 1))
    alone = [second(2 * h, jobs, of[h], ((),) * 4) for h in range(2)]
    got_far = [send(alone[g // 2][g % 2], 1 - g // 2, ways[g]) for g in every]
    got_near = [send(alone[g // 2][2 + g % 2], 1 - g // 2, -ways[g]) for g in every]
    both = [second(2 * h, ((0, 1), (1, -1)), of[h], ((got_far[p],), (got_far[q],))) for h, (p, q) in enumerate(halves)]
    got_both = [send(both[g // 2][g % 2], 1 - g // 2, ways[g]) for g in every]
    states = list(zip(got_near, got_both))
    part = last(0, at, four, table, firsts, states, [], width)
    return last(2, at, four, table, firsts, states, [part], width)


def solution(mesh):
    placed = (P(None, "lat", None, "wave"), P("wave", "lat", None), P("wave"))
    return jax.shard_map(
        per_device, mesh=mesh, in_specs=placed, out_specs=P("lat", "wave", None), check_vma=False
    )
```
